128 devices in a mesh: track: 32 (over y, x, core), strip: 4 (over z).
Axes of the slice: x: 4, y: 4, z: 4, core: 2. Of those that a mesh axis runs over, the one named last changes fastest.
Arguments:
- rhs: float32 [4, 512, 256], P('strip', 'track'), may hold values from -6 to 6
- principal_tiles: bfloat16 [4, 512, 256, 256], P('strip', 'track')
- lower_blocks: bfloat16 [4, 512, 256, 256], P('strip', 'track')
- coupling_blocks: bfloat16 [4, 512, 256, 256], P('strip', 'track'), may hold values from -0.09375 to 0.09375
- precond_blocks: bfloat16 [4, 512, 256, 256], P('strip', 'track'), as said below
- seg_blocks: int32 [32], P('track'), may hold values from 1 to 16, 320 in all
- links: int32 [4, 512], P('strip', 'track'), may hold values 0 or 1
Outputs:
- solution: float32 [4, 512, 256], P('strip', 'track')
- residual: float32 [4, 512, 256], P('strip', 'track')
The draws below stay inside these ranges and needn't reach their ends.
Inputs may be any that keep to these rules, and one draw needn't show every extreme that they name: `seg_blocks`: each device holds at least one live block and the counts of all devices sum to 320. `precond_blocks`: approximate inverses of the diagonal blocks.
All inputs are finite; a program needn't handle non-finite values. No bound on the sum of `links` on one device may be relied on, other than what follows from the above.
Results may differ from the reference program's by a relative error of at most 0.0004.
Values sent between devices are 32-bit elements; how exact they have to be, the bound alone decides.
A program may use at most 128 MiB of HBM per device.

```python
import math
import jax
import jax.numpy as jnp
import numpy as np
from jax import lax

B = 256
CAP = 16
ITERS = 6
BAND_ACTIVE_TILES = 320
N_TRACK = 32
N_STRIP = 4


coupled_noise = 0.25


inverse_noise = 0.1


lower_noise = 0.2


def noise_field(key, tag):
    shape = (N_STRIP, N_TRACK * CAP, B, B)
    sub = jax.random.fold_in(key, tag)
    values = jax.random.normal(sub, shape, jnp.float32)
    return values / math.sqrt(B)


def block_scales(key):
    sub = jax.random.fold_in(key, 21)
    rows = N_TRACK * CAP
    return jnp.exp(jax.random.uniform(sub, (N_STRIP, rows), jnp.float32, math.log(3.0), math.log(8.0)))


def identity_block():
    index = jnp.arange(B)
    return (index[:, None] == index[None, :]).astype(jnp.float32)


def decay_field(key):
    rows = N_TRACK * CAP
    bottom = math.log(0.25 / BAND_ACTIVE_TILES)
    top = math.log(max(0.04, 2.0 / BAND_ACTIVE_TILES))
    falloff_speed = jnp.exp(jax.random.uniform(jax.random.fold_in(key, 31), (N_STRIP, 1, B), jnp.float32, bottom, top))
    extent_across = jnp.exp(jax.random.uniform(jax.random.fold_in(key, 32), (N_STRIP, rows, B), jnp.float32, math.log(0.5), math.log(2.0)))
    chosen_position = jax.random.uniform(jax.random.fold_in(key, 33), (N_STRIP, rows, 1), jnp.float32)
    pass_levels_number = jax.random.uniform(jax.random.fold_in(key, 34), (N_STRIP, rows, 1), jnp.float32, 0.5, 0.8)
    pulse_total = jnp.where(chosen_position < 3.0 / BAND_ACTIVE_TILES, pass_levels_number, 1.0)
    return jnp.exp(-falloff_speed * extent_across) * pulse_total


def draw_principal_tiles(key, part):
    scales = block_scales(key)
    coupled = noise_field(key, 41)
    outcome = scales[:, :, None, None] * (identity_block()[None, None] + coupled_noise * coupled)
    return outcome.astype(jnp.bfloat16)


def draw_precond_blocks(key, part):
    scales = block_scales(key)
    coupled = noise_field(key, 41)
    extra = noise_field(key, 42)
    outcome = (identity_block()[None, None] - coupled_noise * coupled + inverse_noise * extra) / scales[:, :, None, None]
    return outcome.astype(jnp.bfloat16)


def draw_lower_blocks(key, part):
    scales = block_scales(key)
    mixing = noise_field(key, 43)
    decay = decay_field(key)
    norming = math.sqrt((1.0 + coupled_noise ** 2 + inverse_noise ** 2) * (1.0 + lower_noise ** 2))
    outcome = -scales[:, :, None, None] * (identity_block()[None, None] + lower_noise * mixing) * decay[:, :, None, :] / norming
    return outcome.astype(jnp.bfloat16)


def place_ends(drawn, key, low, top_value):
    longest = drawn.shape.index(max(drawn.shape))
    spots = []
    for shift in (0, 1):
        where = [jax.random.randint(jax.random.fold_in(key, axis), (), 0, length) for axis, length in enumerate(drawn.shape)]
        where[longest] = (where[longest] + shift) % drawn.shape[longest]
        spots.append(tuple(where))
    return drawn.at[spots[0]].set(low).at[spots[1]].set(top_value)


def block_levels(rng, shape, shards, least, largest):
    factor_of = 1.0
    for dim, shards_of in shards:
        steps = jax.random.uniform(jax.random.fold_in(jax.random.fold_in(rng, 6), dim), (shards_of,), jnp.float32, least / len(shards), largest / len(shards))
        factor_of = factor_of * jnp.repeat(jnp.exp(steps), shape[dim] // shards_of).reshape((-1,) + (1,) * (len(shape) - 1 - dim))
    return factor_of


def split_up(amount, total, most, lean):
    weights = [(1 << 20) // math.isqrt(standing ** lean) + 1 for standing in range(2, amount + 1)]
    rest, given = total - most - (amount - 1), [1] * (amount - 1)
    while rest > 0:
        movable = [i for i in range(amount - 1) if given[i] < most]
        pool, left = sum([weights[i] for i in movable]), rest
        for i in movable:
            addition = min(most - given[i], max(1, left * weights[i] // pool), rest)
            given[i] = given[i] + addition
            rest = rest - addition
    return np.array([most] + given)


def ragged_sizes(stream_key, count, total, reach, lean):
    if count == 2:
        one = jax.random.randint(stream_key, (), max(1, total - reach), min(reach, total - 1) + 1)
        return jnp.stack([one, total - one])
    tallies = jnp.asarray(split_up(count, total, reach, lean), jnp.int32)
    couples = (count - 1) // 2
    donor, sink = tallies[1:1 + 2 * couples:2], tallies[2:2 + 2 * couples:2]
    margin = jnp.minimum(donor - 1, reach - sink)
    shifted = jax.random.randint(jax.random.fold_in(stream_key, 1), (couples,), 0, 1 << 20) % (margin + 1)
    tallies = tallies.at[1:1 + 2 * couples:2].set(donor - shifted).at[2:2 + 2 * couples:2].set(sink + shifted)
    return tallies[jax.random.permutation(jax.random.fold_in(stream_key, 2), count)]


def scatter_about(rng, extent, scale, bound, cuts=(), kind=jnp.bfloat16):
    array = scale * jax.random.normal(rng, extent, jnp.float32)
    if cuts:
        array = array * block_levels(rng, extent, cuts, -0.22, 0.18)
    return jnp.clip(array, -bound, bound).astype(kind)


def setup_inputs(seed: int = 0) -> dict:
    key_list = jax.random.split(jax.random.key(seed), 8)
    return {
        "rhs": scatter_about(key_list[0], (N_STRIP, N_TRACK * CAP, B), 1.0, 6.0, ((0, 4), (1, 32)), jnp.float32),
        "principal_tiles": draw_principal_tiles(jax.random.fold_in(key_list[7], 71), 0),
        "lower_blocks": draw_lower_blocks(jax.random.fold_in(key_list[7], 71), 0),
        "coupling_blocks": scatter_about(key_list[3], (N_STRIP, N_TRACK * CAP, B, B), (16 * B) ** -0.5, 0.09375, ((0, 4), (1, 32))),
        "precond_blocks": draw_precond_blocks(jax.random.fold_in(key_list[7], 71), 0),
        "seg_blocks": ragged_sizes(key_list[5], N_TRACK, BAND_ACTIVE_TILES, CAP, 2).astype(jnp.int32),
        "links": place_ends((jax.random.randint(key_list[6], (N_STRIP, N_TRACK * CAP), 0, 128) < 127).astype(jnp.int32), jax.random.fold_in(key_list[6], 1), 0, 1),
    }


def apply_blocks(mats, vecs):
    def one(pair):
        return jnp.einsum('kab,kb->ka', pair[0].astype(jnp.float32), pair[1], precision=lax.Precision.HIGHEST)
    return lax.map(one, (mats, vecs))


def apply_transposed(mats, vecs):
    def one(pair):
        return jnp.einsum('kba,kb->ka', pair[0].astype(jnp.float32), pair[1], precision=lax.Precision.HIGHEST)
    return lax.map(one, (mats, vecs))


def reference(rhs, principal_tiles, lower_blocks, coupling_blocks, precond_blocks, seg_blocks, links):
    strips, slots_all, width = rhs.shape
    flat = jnp.arange(slots_all, dtype=jnp.int32)
    slot = flat % CAP
    device = flat // CAP
    count = seg_blocks[device]
    live = slot < count
    prev_count = seg_blocks[jnp.maximum(device - 1, 0)]
    prev_index = jnp.where(slot > 0, flat - 1, (device - 1) * CAP + prev_count - 1)
    prev_index = jnp.clip(prev_index, 0, slots_all - 1).astype(jnp.int32)
    has_prev = live & ((slot > 0) | (device > 0))
    next_index = jnp.where(slot + 1 < count, flat + 1, (device + 1) * CAP)
    next_index = jnp.clip(next_index, 0, slots_all - 1).astype(jnp.int32)
    has_next = live & ((slot + 1 < count) | (device < N_TRACK - 1))
    livef = live.astype(jnp.float32)
    lower_on = links.astype(jnp.float32) * has_prev.astype(jnp.float32)[None, :]
    upper_on = lower_on[:, next_index] * has_next.astype(jnp.float32)[None, :]

    def operate(vec):
        own = apply_blocks(principal_tiles, vec)
        low = apply_blocks(lower_blocks, vec[:, prev_index]) * lower_on[:, :, None]
        up = apply_transposed(lower_blocks, vec)[:, next_index] * upper_on[:, :, None]
        zero = jnp.zeros((1, slots_all, width), jnp.float32)
        below = jnp.concatenate([zero, vec[:-1]], axis=0)
        cross = apply_blocks(coupling_blocks, below)
        back = apply_transposed(coupling_blocks, vec)
        back = jnp.concatenate([back[1:], zero], axis=0)
        return (own + low + up + cross + back) * livef[None, :, None]

    def sweep_strip(precond, lower, resid, on_row):
        def step(prev, item):
            pmat, lmat, rvec, onv, alive = item
            inner = rvec - onv * jnp.dot(lmat.astype(jnp.float32), prev, precision=lax.Precision.HIGHEST)
            value = jnp.dot(pmat.astype(jnp.float32), inner, precision=lax.Precision.HIGHEST)
            return jnp.where(alive > 0, value, prev), value * alive
        _, values = lax.scan(step, jnp.zeros((width,), jnp.float32), (precond, lower, resid, on_row, livef))
        return values

    def precondition(resid):
        return jax.vmap(sweep_strip)(precond_blocks, lower_blocks, resid, lower_on)

    solution = jnp.zeros_like(rhs)
    residual = rhs * livef[None, :, None]
    for step_number in range(ITERS):
        direction = precondition(residual)
        image = operate(direction)
        alpha = jnp.sum(residual * image) / (jnp.sum(image * image) + 1e-6)
        solution = solution + alpha * direction
        residual = residual - alpha * image
    return solution, residual
```

```python
import jax
import jax.numpy as jnp
from jax import lax
from jax.experimental import pallas as pl
from jax.experimental.pallas import tpu as pltpu
from jax.sharding import PartitionSpec as P

ITERS = 6
CAP = 16
W = 256
HALF = 128
NX, NY, NS = 4, 4, 4
NT = 32
MESH = pl.DeviceIdType.MESH
f32, bf16 = jnp.float32, jnp.bfloat16


def split2(x):
    hi = x.astype(bf16)
    return hi, (x - hi.astype(f32)).astype(bf16)


def split3(x):
    hi = x.astype(bf16)
    rest = x - hi.astype(f32)
    mid = rest.astype(bf16)
    lo = (rest - mid.astype(f32)).astype(bf16)
    return jnp.concatenate([hi, mid, lo], axis=0)


def dot(a, b):
    return jnp.dot(a, b, preferred_element_type=f32)


def dot_nt(a, b):
    return lax.dot_general(a, b, (((1,), (1,)), ((), ())), preferred_element_type=f32)


def mm(a, b):
    ah, al = split2(a)
    bh, bl = split2(b)
    return dot(ah, bh) + (dot(al, bh) + dot(ah, bl))


def fold(acc):
    return acc[0:16] + acc[16:32] + acc[32:48]


def eye():
    rows = lax.broadcasted_iota(jnp.int32, (W, W), 0)
    cols = lax.broadcasted_iota(jnp.int32, (W, W), 1)
    return jnp.where(rows == cols, 1.0, 0.0).astype(f32)


def kernel(
    seg, links, rhs, diag_h, low_h, coup_h, pre_h, sol_out, res_out,
    diag, low, coup, pre, diag_t, low_t, coup_t, pre_t,
    steps, prefix, ends, scans, tails,
    own, other, chip, xm, row, ym, work,
    hot, msg, got, smsg, sgot, up_buf, up_got, down_buf, down_got, edge_buf, edge_got,
    vst, loc, prevs, shifts, x_s, r_s, z_s, w_s, q_s,
    load_sem, pair_sem, sx_sem, rx_sem, sf_sem, rf_sem, sy_sem, ry_sem, sg_sem, rg_sem,
    gs_sem, gr_sem, ss_sem, sr_sem, hs_sem, hr_sem,
):
    t = lax.axis_index("track")
    s = lax.axis_index("strip")
    core = lax.rem(t, 2)
    x = lax.rem(t // 2, NX)
    y = t // (2 * NX)
    mate = t + 1 - 2 * core

    loads = [
        pltpu.make_async_copy(low_h, low, load_sem.at[0]),
        pltpu.make_async_copy(pre_h, pre, load_sem.at[1]),
        pltpu.make_async_copy(coup_h, coup, load_sem.at[2]),
        pltpu.make_async_copy(diag_h, diag, load_sem.at[3]),
    ]
    for copy in loads:
        copy.start()

    barrier = pltpu.get_barrier_semaphore()

    def greet(i, _):
        pl.semaphore_signal(
            barrier, inc=1, device_id=(lax.rem(t + i, NT), s), device_id_type=MESH
        )
        return 0

    lax.fori_loop(1, NT, greet, 0)
    for i in range(1, NS):
        pl.semaphore_signal(
            barrier, inc=1, device_id=(t, lax.rem(s + i, NS)), device_id_type=MESH
        )

    count = seg[0]
    slot = lax.broadcasted_iota(jnp.int32, (CAP, W), 0)
    live = jnp.where(slot < count, 1.0, 0.0).astype(f32)
    at_end = jnp.where(slot == count - 1, 1.0, 0.0).astype(f32)
    slots48 = lax.rem(lax.broadcasted_iota(jnp.int32, (48, W), 0), CAP)
    for j in range(CAP):
        hot[j] = jnp.where(slots48 == j, 1.0, 0.0).astype(bf16)
    r_s[...] = rhs[...] * live
    q_s[...] = rhs[...] * live
    for ref in (x_s, z_s, w_s, msg, vst, shifts):
        ref[...] = jnp.zeros_like(ref)

    loads[0].wait()
    loads[1].wait()

    def make_step(j, _):
        alive = jnp.where(j < count, 1.0, 0.0).astype(f32)
        linked = links[0, j].astype(f32) * alive * jnp.where(j + t > 0, 1.0, 0.0).astype(f32)
        lower = low[j].astype(f32) * linked
        low[j] = lower.astype(bf16)
        low_t[j] = lower.T.astype(bf16)
        pre[j] = (pre[j].astype(f32) * alive).astype(bf16)
        step = (1.0 - alive) * eye() - dot_nt(low_t[j], pre[j])
        hi, lo = split2(step)
        steps[j, 0] = hi
        steps[j, 1] = lo
        return 0

    lax.fori_loop(0, CAP, make_step, 0)

    prefix[0, 0] = steps[0, 0]
    prefix[0, 1] = steps[0, 1]

    def make_prefix(j, _):
        ah, al = prefix[j - 1, 0], prefix[j - 1, 1]
        bh, bl = steps[j, 0], steps[j, 1]
        value = dot(ah, bh) + (dot(al, bh) + dot(ah, bl))
        own[...] = value
        hi, lo = split2(value)
        prefix[j, 0] = hi
        prefix[j, 1] = lo
        return 0

    lax.fori_loop(1, CAP, make_prefix, 0)

    pl.semaphore_wait(barrier, NT - 1 + NS - 1)

    def remote(src, dst, send, recv, tt, ss):
        return pltpu.make_async_remote_copy(
            src_ref=src, dst_ref=dst, send_sem=send, recv_sem=recv,
            device_id=(tt, ss), device_id_type=MESH,
        )

    pair = remote(own, other, pair_sem.at[0], pair_sem.at[1], mate, s)
    pair.start()
    loads[2].wait()
    loads[3].wait()

    def flip_pre(j, _):
        pre_t[j] = pre[j].astype(f32).T.astype(bf16)
        return 0

    lax.fori_loop(0, CAP, flip_pre, 0)
    pair.wait()
    first = core == 0
    chip[...] = mm(
        jnp.where(first, own[...], other[...]), jnp.where(first, other[...], own[...])
    )

    half = pl.ds(pl.multiple_of(core * HALF, HALF), HALF)

    def ring_start(src, dst, send, recv, pos, stride):
        copies = []
        for i in range(1, 4):
            to = t + (lax.rem(pos + i, 4) - pos) * stride
            c = remote(src.at[half], dst.at[pos, half], send.at[i - 1], recv.at[i - 1], to, s)
            c.start()
            copies.append(c)
        return copies

    def ring_end(copies, dst, fsend, frecv, pos):
        swaps = []
        for i in range(1, 4):
            copies[i - 1].wait_recv()
            at = lax.rem(pos + 4 - i, 4)
            c = remote(dst.at[at, half], dst.at[at, half], fsend.at[i - 1], frecv.at[i - 1], mate, s)
            c.start()
            swaps.append(c)
        for c in swaps:
            c.wait()
        for c in copies:
            c.wait_send()

    copies = ring_start(chip, xm, sx_sem, rx_sem, x, 2)
    xm[x] = chip[...]

    work[...] = eye()

    def make_ends(n, _):
        j = CAP - 1 - n
        hi, lo = split2(work[...])
        ends[j, 0], ends[j, 1] = split2(dot(pre_t[j], hi) + dot(pre_t[j], lo))
        ah, al = steps[j, 0], steps[j, 1]
        work[...] = dot(ah, hi) + (dot(al, hi) + dot(ah, lo))
        return 0

    lax.fori_loop(0, CAP, make_ends, 0)

    ring_end(copies, xm, sf_sem, rf_sem, x)
    row[...] = mm(mm(xm[0], xm[1]), mm(xm[2], xm[3]))
    copies = ring_start(row, ym, sy_sem, ry_sem, y, 2 * NX)
    ym[y] = row[...]

    ident = eye()
    one = lambda flag: jnp.where(flag, 1.0, 0.0).astype(f32)
    enter = jnp.where(first, ident, other[...])
    leave = jnp.where(first, other[...], ident)
    work[...] = mm(jnp.where(x > 1, xm[1], ident), jnp.where(x > 2, xm[2], ident))
    scans[3, 0], scans[3, 1] = split2(mm(work[...], enter) * one(x > 0))
    scans[4, 0], scans[4, 1] = split2(mm(jnp.where(x > 2, xm[2], ident), enter) * one(x > 1))
    scans[5, 0], scans[5, 1] = split2(enter * one(x > 2))
    work[...] = mm(mm(jnp.where(x > 0, xm[0], ident), work[...]), enter)
    tails[0, 0], tails[0, 1] = split2(leave)
    chip[...] = mm(
        mm(jnp.where(x < 1, xm[1], ident), jnp.where(x < 2, xm[2], ident)),
        jnp.where(x < 3, xm[3], ident),
    )
    tails[1, 0], tails[1, 1] = split2(mm(leave, chip[...]))

    def flip_rest(j, _):
        diag_t[j] = diag[j].astype(f32).T.astype(bf16)
        coup_t[j] = coup[j].astype(f32).T.astype(bf16)
        return 0

    lax.fori_loop(0, CAP, flip_rest, 0)

    ring_end(copies, ym, sg_sem, rg_sem, y)
    later = jnp.where(y > 2, ym[2], ident)
    row[...] = mm(jnp.where(y > 1, ym[1], ident), later)
    scans[0, 0], scans[0, 1] = split2(mm(row[...], work[...]) * one(y > 0))
    scans[1, 0], scans[1, 1] = split2(mm(later, work[...]) * one(y > 1))
    scans[2, 0], scans[2, 1] = split2(work[...] * one(y > 2))

    def each_slot(vec, mats):
        parts = split3(vec)
        acc = jnp.zeros((48, W), f32)
        for j in range(CAP):
            acc = acc + dot(parts * hot[j], mats[j])
        return acc

    def each_slot2(vec, mats, n):
        parts = split3(vec)
        acc = jnp.zeros((48, W), f32)
        for j in range(n):
            mine = parts * hot[j]
            acc = acc + dot(mine, mats[j, 0])
            acc = acc + dot(mine, mats[j, 1])
        return acc

    def exchange_start(par):
        for i in range(1, NT):
            to = lax.rem(t + i, NT)
            ty, tx = to // (2 * NX), to // 2
            kind = jnp.where(ty != y, 2, jnp.where(tx != t // 2, 1, 0))
            remote(
                msg.at[par, kind], got.at[par, NT - i - 1], gs_sem.at[par], gr_sem.at[par], to, s
            ).start()

    def exchange_end(par):
        whole = got.at[par]
        pltpu.make_async_copy(whole, whole, gr_sem.at[par]).wait()
        pltpu.make_async_copy(whole, whole, gs_sem.at[par]).wait()

    def strips_start(par):
        total = msg[par, 0]
        for i in range(NT - 1):
            total = total + got[par, i]
        smsg[par] = total
        out = []
        for i in range(1, NS):
            c = remote(
                smsg.at[par], sgot.at[par, i - 1], ss_sem.at[par, i - 1], sr_sem.at[par, i - 1],
                t, lax.rem(s + i, NS),
            )
            c.start()
            out.append(c)
        return out

    def strips_end(par, out):
        for c in out:
            c.wait()
        total = smsg[par] + sgot[par, 0] + sgot[par, 1] + sgot[par, 2]
        inner = jnp.sum(total[2:3], axis=1, keepdims=True)
        energy = jnp.sum(total[3:4], axis=1, keepdims=True)
        return inner / (energy + 1e-6)

    def put_sums(par):
        prod = r_s[...] * w_s[...]
        square = w_s[...] * w_s[...]
        prod = jnp.sum(prod, axis=0, keepdims=True)
        square = jnp.sum(square, axis=0, keepdims=True)
        prod = prod[:, :HALF] + prod[:, HALF:]
        square = square[:, :HALF] + square[:, HALF:]
        for kind in range(3):
            msg[par, kind, 2:3] = prod
            msg[par, kind, 3:4] = square

    def put_vec(par, kind, vec):
        msg[par, kind, 0:1] = vec[:, :HALF]
        msg[par, kind, 1:2] = vec[:, HALF:]

    def iteration(k, _):
        par = lax.rem(k, 2)
        put_sums(par)
        vec = q_s[...]
        end = jnp.sum(each_slot2(vec, ends, CAP), axis=0, keepdims=True)
        parts = split3(end)
        put_vec(par, 0, end)
        for kind in range(2):
            out = dot(parts, tails[kind, 0]) + dot(parts, tails[kind, 1])
            put_vec(par, kind + 1, jnp.sum(out, axis=0, keepdims=True))
        exchange_start(par)

        loc[...] = fold(each_slot(vec, pre_t))
        prev = loc[0:1]
        for j in range(1, CAP):
            parts = split3(prev)
            out = dot(parts, steps[j, 0]) + dot(parts, steps[j, 1])
            prev = loc[j : j + 1] + jnp.sum(out, axis=0, keepdims=True)
            loc[j : j + 1] = prev

        exchange_end(par)
        sums = strips_start(par)

        def message(source):
            return got[par, jnp.maximum(lax.rem(source - t + NT, NT) - 1, 0)]

        for c in range(3):
            total = message(c * 2 * NX)
            for i in range(1, 2 * NX):
                total = total + message(c * 2 * NX + i)
            vst[c : c + 1, :HALF] = total[0:1]
            vst[c : c + 1, HALF:] = total[1:2]
        for c in range(3):
            base = y * 2 * NX + 2 * c
            total = message(base) + message(base + 1)
            vst[c + 3 : c + 4, :HALF] = total[0:1]
            vst[c + 3 : c + 4, HALF:] = total[1:2]
        near = got[par, NT - 2]
        near = jnp.concatenate([near[0:1], near[1:2]], axis=1)
        entry = jnp.sum(each_slot2(vst[...], scans, 6), axis=0, keepdims=True)
        entry = entry + jnp.where(first, jnp.zeros_like(near), near)

        carried = fold(each_slot2(jnp.broadcast_to(entry, (CAP, W)), prefix, CAP))
        step = (loc[...] + carried) * live
        up_buf[par] = step
        up = remote(
            up_buf.at[par], up_got.at[par], hs_sem.at[par, 0], hr_sem.at[par, 0],
            t, lax.rem(s + 1, NS),
        )
        up.start()
        lifted = fold(each_slot(step, low))
        shifts[0:CAP] = lifted
        edge_buf[par] = lifted[0:1]
        edge = remote(
            edge_buf.at[par], edge_got.at[par], hs_sem.at[par, 1], hr_sem.at[par, 1],
            lax.rem(t + NT - 1, NT), s,
        )
        edge.start()
        down_buf[par] = fold(each_slot(step, coup))
        down = remote(
            down_buf.at[par], down_got.at[par], hs_sem.at[par, 2], hr_sem.at[par, 2],
            t, lax.rem(s + NS - 1, NS),
        )
        down.start()
        prevs[0:1] = entry
        prevs[1 : CAP + 1] = step
        total = fold(each_slot(step, diag_t) + each_slot(prevs[0:CAP], low_t)) + shifts[1 : CAP + 1]
        alpha = strips_end(par, sums)
        alpha = jnp.broadcast_to(alpha, (CAP, W))
        start = k == 0
        r_s[...] = r_s[...] - jnp.where(start, 0.0, alpha * w_s[...])
        x_s[...] = x_s[...] + jnp.where(start, 0.0, alpha * z_s[...])
        z_s[...] = jnp.where(start, step, z_s[...] - alpha * step)
        up.wait()
        zero = jnp.zeros((CAP, W), f32)
        below = jnp.where(s > 0, up_got[par], zero)
        total = total + fold(each_slot(below, coup_t))
        edge.wait()
        down.wait()
        total = total + jnp.where(s < NS - 1, down_got[par], zero)
        nxt = jnp.broadcast_to(edge_got[par], (CAP, W))
        total = (total + at_end * jnp.where(t < NT - 1, nxt, zero)) * live
        image = jnp.where(start, total, w_s[...] - alpha * total)
        w_s[...] = image
        q_s[...] = image
        return 0

    lax.fori_loop(0, ITERS, iteration, 0)
    par = ITERS % 2
    put_sums(par)
    exchange_start(par)
    exchange_end(par)
    alpha = jnp.broadcast_to(strips_end(par, strips_start(par)), (CAP, W))
    sol_out[...] = x_s[...] + alpha * z_s[...]
    res_out[...] = r_s[...] - alpha * w_s[...]


def body(rhs, diag, low, coup, pre, seg, links):
    vmem = pl.BlockSpec(memory_space=pltpu.VMEM)
    smem = pl.BlockSpec(memory_space=pltpu.SMEM)
    anyw = pl.BlockSpec(memory_space=pl.ANY)
    mats = pltpu.VMEM((CAP, W, W), bf16)
    mats2 = pltpu.VMEM((CAP, 2, W, W), bf16)
    big = pltpu.VMEM((W, W), f32)
    big4 = pltpu.VMEM((4, W, W), f32)
    vec = pltpu.VMEM((CAP, W), f32)
    dma = pltpu.SemaphoreType.DMA
    out = jax.ShapeDtypeStruct((CAP, W), f32)
    sol, res = pl.pallas_call(
        kernel,
        out_shape=(out, out),
        in_specs=[smem, smem, vmem, anyw, anyw, anyw, anyw],
        out_specs=(vmem, vmem),
        scratch_shapes=[mats] * 8
        + [
            mats2, mats2, mats2,
            pltpu.VMEM((6, 2, W, W), bf16), pltpu.VMEM((2, 2, W, W), bf16),
            big, big, big, big4, big, big4, big,
            pltpu.VMEM((CAP, 48, W), bf16),
            pltpu.VMEM((2, 3, 4, HALF), f32), pltpu.VMEM((2, NT - 1, 4, HALF), f32),
            pltpu.VMEM((2, 4, HALF), f32), pltpu.VMEM((2, NS - 1, 4, HALF), f32),
            pltpu.VMEM((2, CAP, W), f32), pltpu.VMEM((2, CAP, W), f32),
            pltpu.VMEM((2, CAP, W), f32), pltpu.VMEM((2, CAP, W), f32),
            pltpu.VMEM((2, 1, W), f32), pltpu.VMEM((2, 1, W), f32),
            vec, vec, pltpu.VMEM((CAP + 8, W), f32), pltpu.VMEM((CAP + 8, W), f32),
            vec, vec, vec, vec, vec,
            dma((4,)), dma((2,)), dma((3,)), dma((3,)), dma((3,)), dma((3,)),
            dma((3,)), dma((3,)), dma((3,)), dma((3,)),
            dma((2,)), dma((2,)), dma((2, 3)), dma((2, 3)), dma((2, 3)), dma((2, 3)),
        ],
        compiler_params=pltpu.CompilerParams(
            collective_id=0, has_side_effects=True, vmem_limit_bytes=58 * 1024 * 1024
        ),
        name="solve",
    )(seg, links, rhs[0], diag[0], low[0], coup[0], pre[0])
    return sol[None], res[None]


def solution(mesh):
    in_specs = (
        P("strip", "track", None),
        P("strip", "track", None, None),
        P("strip", "track", None, None),
        P("strip", "track", None, None),
        P("strip", "track", None, None),
        P("track"),
        P("strip", "track"),
    )
    out_specs = (P("strip", "track", None), P("strip", "track", None))
    return jax.shard_map(body, mesh=mesh, in_specs=in_specs, out_specs=out_specs, check_vma=False)
```

```python
import jax
import jax.numpy as jnp
from jax import lax
from jax.experimental import pallas as pl
from jax.experimental.pallas import tpu as pltpu
from jax.sharding import PartitionSpec as P

ITERS = 6
CAP = 16
W = 256
HALF = 128
NX, NY, NS = 4, 4, 4
NT = 32
MESH = pl.DeviceIdType.MESH
f32, bf16 = jnp.float32, jnp.bfloat16


def split2(x):
    hi = x.astype(bf16)
    return hi, (x - hi.astype(f32)).astype(bf16)


def split3(x):
    hi = x.astype(bf16)
    rest = x - hi.astype(f32)
    mid = rest.astype(bf16)
    lo = (rest - mid.astype(f32)).astype(bf16)
    return jnp.concatenate([hi, mid, lo], axis=0)


def dot(a, b):
    return jnp.dot(a, b, preferred_element_type=f32)


def dot_nt(a, b):
    return lax.dot_general(a, b, (((1,), (1,)), ((), ())), preferred_element_type=f32)


def mm(a, b):
    ah, al = split2(a)
    bh, bl = split2(b)
    return dot(ah, bh) + (dot(al, bh) + dot(ah, bl))


def fold(acc):
    return acc[0:16] + acc[16:32] + acc[32:48]


def flip(mat):
    return dot_nt(eye().astype(bf16), mat).astype(bf16)


def eye():
    rows = lax.broadcasted_iota(jnp.int32, (W, W), 0)
    cols = lax.broadcasted_iota(jnp.int32, (W, W), 1)
    return jnp.where(rows == cols, 1.0, 0.0).astype(f32)


def kernel(
    seg, links, rhs, diag_h, low_h, coup_h, pre_h, sol_out, res_out,
    diag, low, coup, pre, diag_t, low_t, coup_t, pre_t,
    steps, prefix, ends, scans, tails,
    own, other, chip, xm, row, ym, work,
    hot, msg, got, smsg, sgot, up_buf, up_got, down_buf, down_got, edge_buf, edge_got,
    group, column, car, loc, prevs, shifts, x_s, r_s, z_s, w_s, q_s,
    load_sem, pair_sem, sx_sem, rx_sem, sf_sem, rf_sem, sy_sem, ry_sem,
    gs_sem, gr_sem, ss_sem, sr_sem, hs_sem, hr_sem,
):
    t = lax.axis_index("track")
    s = lax.axis_index("strip")
    core = lax.rem(t, 2)
    x = lax.rem(t // 2, NX)
    y = t // (2 * NX)
    mate = t + 1 - 2 * core

    loads = [
        pltpu.make_async_copy(low_h, low, load_sem.at[0]),
        pltpu.make_async_copy(pre_h, pre, load_sem.at[1]),
        pltpu.make_async_copy(coup_h, coup, load_sem.at[2]),
        pltpu.make_async_copy(diag_h, diag, load_sem.at[3]),
    ]
    for copy in loads:
        copy.start()

    ym[...] = jnp.zeros_like(ym)
    barrier = pltpu.get_barrier_semaphore()

    def greet(i, _):
        pl.semaphore_signal(
            barrier, inc=1, device_id=(lax.rem(t + i, NT), s), device_id_type=MESH
        )
        return 0

    lax.fori_loop(1, NT, greet, 0)
    for i in range(1, NS):
        pl.semaphore_signal(
            barrier, inc=1, device_id=(t, lax.rem(s + i, NS)), device_id_type=MESH
        )

    count = seg[0]
    slot = lax.broadcasted_iota(jnp.int32, (CAP, W), 0)
    live = jnp.where(slot < count, 1.0, 0.0).astype(f32)
    at_end = jnp.where(slot == count - 1, 1.0, 0.0).astype(f32)
    slots48 = lax.rem(lax.broadcasted_iota(jnp.int32, (48, W), 0), CAP)
    for j in range(CAP):
        hot[j] = jnp.where(slots48 == j, 1.0, 0.0).astype(bf16)
    r_s[...] = rhs[...] * live
    q_s[...] = rhs[...] * live
    for ref in (x_s, z_s, w_s, msg, shifts):
        ref[...] = jnp.zeros_like(ref)

    loads[0].wait()
    loads[1].wait()

    def make_step(j, _):
        alive = jnp.where(j < count, 1.0, 0.0).astype(f32)
        linked = links[0, j].astype(f32) * alive * jnp.where(j + t > 0, 1.0, 0.0).astype(f32)
        lower = (low[j].astype(f32) * linked).astype(bf16)
        inverse = (pre[j].astype(f32) * alive).astype(bf16)
        lower_t = flip(lower)
        low[j] = lower
        low_t[j] = lower_t
        pre[j] = inverse
        steps[j, 0], steps[j, 1] = split2((1.0 - alive) * eye() - dot_nt(lower_t, inverse))
        return 0

    lax.fori_loop(0, CAP, make_step, 0, unroll=2)

    for g in range(4):
        prefix[4 * g] = steps[4 * g, 0].astype(f32) + steps[4 * g, 1].astype(f32)

    def make_prefix(n, _):
        for g in range(4):
            j = 4 * g + n
            ah, al = split2(prefix[j - 1])
            bh, bl = steps[j, 0], steps[j, 1]
            prefix[j] = dot(ah, bh) + (dot(al, bh) + dot(ah, bl))
        return 0

    lax.fori_loop(1, 4, make_prefix, 0)
    group[0] = mm(prefix[3], prefix[7])
    own[...] = mm(group[0], mm(prefix[11], prefix[15]))

    pl.semaphore_wait(barrier, NT - 1 + NS - 1)

    def remote(src, dst, send, recv, tt, ss):
        return pltpu.make_async_remote_copy(
            src_ref=src, dst_ref=dst, send_sem=send, recv_sem=recv,
            device_id=(tt, ss), device_id_type=MESH,
        )

    pair = remote(own, other, pair_sem.at[0], pair_sem.at[1], mate, s)
    pair.start()
    loads[2].wait()
    loads[3].wait()

    def flip_pre(j, _):
        pre_t[j] = flip(pre[j])
        return 0

    lax.fori_loop(0, CAP, flip_pre, 0, unroll=2)
    pair.wait()
    first = core == 0
    chip[...] = mm(
        jnp.where(first, own[...], other[...]), jnp.where(first, other[...], own[...])
    )

    half = pl.ds(pl.multiple_of(core * HALF, HALF), HALF)

    copies = []
    for i in (2, 1, 3):
        to = t + (lax.rem(x + i, NX) - x) * 2
        c = remote(chip.at[half], xm.at[x, half], sx_sem.at[i - 1], rx_sem.at[i - 1], to, s)
        c.start()
        copies.append((i, c))
    xm[x] = chip[...]

    group[1] = mm(group[0], prefix[11])

    def join_prefix(n, _):
        for g in range(1, 4):
            before = prefix[3] if g == 1 else group[g - 2]
            prefix[4 * g + n] = mm(before, prefix[4 * g + n])
        return 0

    lax.fori_loop(0, 4, join_prefix, 0)

    work[...] = eye()

    def make_ends(n, _):
        j = CAP - 1 - n
        alive = jnp.where(j < count, 1.0, 0.0).astype(f32)
        hi, lo = split2(work[...])
        ends[j] = dot(hi, pre[j]) + dot(lo, pre[j])
        bh, bl = split2((1.0 - alive) * eye() - dot(pre[j], low[j]))
        work[...] = dot(hi, bh) + (dot(lo, bh) + dot(hi, bl))
        return 0

    lax.fori_loop(0, CAP, make_ends, 0)

    def flip_rest(j, _):
        diag_t[j] = flip(diag[j])
        coup_t[j] = flip(coup[j])
        return 0

    lax.fori_loop(0, CAP, flip_rest, 0, unroll=2)

    swaps = []
    for i, c in copies[1:] + copies[:1]:
        c.wait_recv()
        at = lax.rem(x + NX - i, NX)
        c = remote(xm.at[at, half], xm.at[at, half], sf_sem.at[i - 1], rf_sem.at[i - 1], mate, s)
        c.start()
        swaps.append(c)
    for c in swaps:
        c.wait()
    for i, c in copies:
        c.wait_send()

    row[...] = mm(mm(xm[0], xm[1]), mm(xm[2], xm[3]))
    giver = (y == 1) | (y == 2)
    taker = (y == 0) | (y == 3)
    far = jnp.where(y == 1, t - 2 * NX, jnp.where(y == 2, t + 2 * NX, t))
    hop = remote(row.at[half], ym.at[half], sy_sem.at[0], ry_sem.at[0], far, s)

    @pl.when(giver)
    def _():
        hop.start()

    ident = eye()
    one = lambda flag: jnp.where(flag, 1.0, 0.0).astype(f32)
    enter = jnp.where(first, ident, other[...])
    leave = jnp.where(first, other[...], ident)
    work[...] = mm(jnp.where(x > 1, xm[1], ident), jnp.where(x > 2, xm[2], ident))
    scans[2] = (enter * one(x > 0)).T
    behind = xm[lax.rem(x + 3, NX)]
    scans[3] = (mm(behind, enter) * one(x > 1)).T
    scans[4] = (mm(mm(xm[lax.rem(x + 2, NX)], behind), enter) * one(x > 2)).T
    scans[5] = ident * one(core > 0)
    work[...] = mm(mm(jnp.where(x > 0, xm[0], ident), work[...]), enter)
    scans[0] = (work[...] * one(y > 0)).T
    tails[0] = ident
    tails[1] = leave
    chip[...] = mm(
        mm(jnp.where(x < 1, xm[1], ident), jnp.where(x < 2, xm[2], ident)),
        jnp.where(x < 3, xm[3], ident),
    )
    own[...] = mm(leave, chip[...])
    tails[2] = own[...]

    @pl.when(giver)
    def _():
        hop.wait_send()

    @pl.when(taker)
    def _():
        hop.wait_recv()
        c = remote(ym.at[half], ym.at[half], sy_sem.at[1], ry_sem.at[1], mate, s)
        c.start()
        c.wait()

    over = mm(jnp.where(y == 0, own[...], ym[...]), jnp.where(y == 0, ym[...], work[...]))
    scans[1] = (over * one(y == 3)).T
    tails[3] = jnp.where(y == 0, over, own[...])

    def each_slot(vec, mats):
        parts = split3(vec)
        acc = jnp.zeros((48, W), f32)
        for j in range(CAP):
            acc = acc + dot(parts * hot[j], mats[j])
        return acc

    def to_column(vecs, mats):
        for b in range(0, W, 8):
            left = right = None
            for i, (v0, v1) in enumerate(vecs):
                p0 = mats[i, b : b + 8, :HALF] * v0
                p1 = mats[i, b : b + 8, HALF:] * v1
                left = p0 if left is None else left + p0
                right = p1 if right is None else right + p1
            total = jnp.sum(left + right, axis=1, keepdims=True)
            column[b : b + 8] = jnp.broadcast_to(total, (8, HALF))

    def to_row(mats, j):
        left = right = None
        for b in range(0, W, 8):
            part = column[b : b + 8]
            p0 = part * mats[j, b : b + 8, :HALF]
            p1 = part * mats[j, b : b + 8, HALF:]
            left = p0 if left is None else left + p0
            right = p1 if right is None else right + p1
        return jnp.sum(left, axis=0, keepdims=True), jnp.sum(right, axis=0, keepdims=True)

    wide = lambda row: jnp.broadcast_to(row, (8, HALF))

    hops = lambda d: min(d, 4 - d)
    places = [(dy, dx, dc) for dy in range(NY) for dx in range(NX) for dc in range(2)][1:]
    places.sort(key=lambda p: -(2 * (hops(p[0]) + hops(p[1])) + p[2]))
    routes = []
    for dy, dx, dc in places:
        to = lax.rem(y + dy, NY) * 2 * NX + lax.rem(x + dx, NX) * 2 + lax.rem(core + dc, 2)
        kind = 3 if dy > 1 else 2 if dy else 1 if dx else 0
        at = (-dy % NY) * 2 * NX + (-dx % NX) * 2 + dc - 1
        routes.append((to, kind, at))

    def exchange_start(par):
        for to, kind, at in routes:
            remote(
                msg.at[par, kind], got.at[par, at], gs_sem.at[par], gr_sem.at[par], to, s
            ).start()

    def exchange_end(par):
        whole = got.at[par]
        pltpu.make_async_copy(whole, whole, gr_sem.at[par]).wait()
        pltpu.make_async_copy(whole, whole, gs_sem.at[par]).wait()

    def class_sums(par):
        rows = []
        for d in range(1, NY):
            first_at = (NY - d) * 2 * NX - 1
            total = got[par, first_at]
            for i in range(1, 2 * NX):
                total = total + got[par, first_at + i]
            rows.append(total)
        cols = [
            got[par, (NX - d) * 2 - 1] + got[par, (NX - d) * 2] for d in range(1, NX)
        ]
        return rows, cols, got[par, 0]

    def strips_start(par, rows, cols, near):
        total = msg[par, 0] + near
        for part in rows + cols:
            total = total + part
        smsg[par] = total
        out = []
        for i in range(1, NS):
            c = remote(
                smsg.at[par], sgot.at[par, i - 1], ss_sem.at[par, i - 1], sr_sem.at[par, i - 1],
                t, lax.rem(s + i, NS),
            )
            c.start()
            out.append(c)
        return out

    def strips_end(par, out):
        for c in out:
            c.wait()
        total = smsg[par] + sgot[par, 0] + sgot[par, 1] + sgot[par, 2]
        inner = jnp.sum(total[2:3], axis=1, keepdims=True)
        energy = jnp.sum(total[3:4], axis=1, keepdims=True)
        return inner / (energy + 1e-6)

    def put_sums(par):
        prod = r_s[...] * w_s[...]
        square = w_s[...] * w_s[...]
        prod = jnp.sum(prod, axis=0, keepdims=True)
        square = jnp.sum(square, axis=0, keepdims=True)
        prod = prod[:, :HALF] + prod[:, HALF:]
        square = square[:, :HALF] + square[:, HALF:]
        for kind in range(4):
            msg[par, kind, 2:3] = prod
            msg[par, kind, 3:4] = square

    def iteration(k, _):
        par = lax.rem(k, 2)
        put_sums(par)
        vec = q_s[...]
        to_column(
            [(wide(q_s[i : i + 1, :HALF]), wide(q_s[i : i + 1, HALF:])) for i in range(CAP)], ends
        )
        for kind in range(4):
            msg[par, kind, 0:1], msg[par, kind, 1:2] = to_row(tails, kind)
        exchange_start(par)

        loc[...] = fold(each_slot(vec, pre_t))
        prev = loc[0:1]
        for j in range(1, CAP):
            parts = split3(prev)
            out = dot(parts, steps[j, 0]) + dot(parts, steps[j, 1])
            prev = loc[j : j + 1] + jnp.sum(out, axis=0, keepdims=True)
            loc[j : j + 1] = prev

        exchange_end(par)
        rows, cols, near = class_sums(par)
        sums = strips_start(par, rows, cols, near)
        heads = [rows[0] + rows[1] * one(y == 2), rows[1] + rows[2]] + cols + [near]
        to_column([(wide(h[0:1]), wide(h[1:2])) for h in heads], scans)
        for j in range(CAP):
            car[j : j + 1, :HALF], car[j : j + 1, HALF:] = to_row(prefix, j)
        prevs[0:1, :HALF], prevs[0:1, HALF:] = to_row(tails, 0)
        step = (loc[...] + car[...]) * live
        up_buf[par] = step
        up = remote(
            up_buf.at[par], up_got.at[par], hs_sem.at[par, 0], hr_sem.at[par, 0],
            t, lax.rem(s + 1, NS),
        )
        up.start()
        edge_row = dot(split3(step) * hot[0], low[0])
        edge_buf[par] = jnp.sum(edge_row, axis=0, keepdims=True)
        edge = remote(
            edge_buf.at[par], edge_got.at[par], hs_sem.at[par, 1], hr_sem.at[par, 1],
            lax.rem(t + NT - 1, NT), s,
        )
        edge.start()
        down_buf[par] = fold(each_slot(step, coup))
        down = remote(
            down_buf.at[par], down_got.at[par], hs_sem.at[par, 2], hr_sem.at[par, 2],
            t, lax.rem(s + NS - 1, NS),
        )
        down.start()
        shifts[0:CAP] = fold(each_slot(step, low))
        prevs[1 : CAP + 1] = step
        total = fold(each_slot(step, diag_t) + each_slot(prevs[0:CAP], low_t)) + shifts[1 : CAP + 1]
        alpha = strips_end(par, sums)
        alpha = jnp.broadcast_to(alpha, (CAP, W))
        start = k == 0
        r_s[...] = r_s[...] - jnp.where(start, 0.0, alpha * w_s[...])
        x_s[...] = x_s[...] + jnp.where(start, 0.0, alpha * z_s[...])
        z_s[...] = jnp.where(start, step, z_s[...] - alpha * step)
        up.wait()
        zero = jnp.zeros((CAP, W), f32)
        below = jnp.where(s > 0, up_got[par], zero)
        total = total + fold(each_slot(below, coup_t))
        edge.wait()
        down.wait()
        total = total + jnp.where(s < NS - 1, down_got[par], zero)
        nxt = jnp.broadcast_to(edge_got[par], (CAP, W))
        total = (total + at_end * jnp.where(t < NT - 1, nxt, zero)) * live
        image = jnp.where(start, total, w_s[...] - alpha * total)
        w_s[...] = image
        q_s[...] = image
        return 0

    lax.fori_loop(0, ITERS, iteration, 0)
    par = ITERS % 2
    put_sums(par)
    exchange_start(par)
    exchange_end(par)
    alpha = jnp.broadcast_to(strips_end(par, strips_start(par, *class_sums(par))), (CAP, W))
    sol_out[...] = x_s[...] + alpha * z_s[...]
    res_out[...] = r_s[...] - alpha * w_s[...]


def body(rhs, diag, low, coup, pre, seg, links):
    vmem = pl.BlockSpec(memory_space=pltpu.VMEM)
    smem = pl.BlockSpec(memory_space=pltpu.SMEM)
    anyw = pl.BlockSpec(memory_space=pl.ANY)
    mats = pltpu.VMEM((CAP, W, W), bf16)
    mats2 = pltpu.VMEM((CAP, 2, W, W), bf16)
    big = pltpu.VMEM((W, W), f32)
    big4 = pltpu.VMEM((4, W, W), f32)
    vec = pltpu.VMEM((CAP, W), f32)
    dma = pltpu.SemaphoreType.DMA
    out = jax.ShapeDtypeStruct((CAP, W), f32)
    sol, res = pl.pallas_call(
        kernel,
        out_shape=(out, out),
        in_specs=[smem, smem, vmem, anyw, anyw, anyw, anyw],
        out_specs=(vmem, vmem),
        scratch_shapes=[mats] * 8
        + [
            mats2, pltpu.VMEM((CAP, W, W), f32), pltpu.VMEM((CAP, W, W), f32),
            pltpu.VMEM((6, W, W), f32), pltpu.VMEM((4, W, W), f32),
            big, big, big, big4, big, big, big,
            pltpu.VMEM((CAP, 48, W), bf16),
            pltpu.VMEM((2, 4, 4, HALF), f32), pltpu.VMEM((2, NT - 1, 4, HALF), f32),
            pltpu.VMEM((2, 4, HALF), f32), pltpu.VMEM((2, NS - 1, 4, HALF), f32),
            pltpu.VMEM((2, CAP, W), f32), pltpu.VMEM((2, CAP, W), f32),
            pltpu.VMEM((2, CAP, W), f32), pltpu.VMEM((2, CAP, W), f32),
            pltpu.VMEM((2, 1, W), f32), pltpu.VMEM((2, 1, W), f32),
            pltpu.VMEM((2, W, W), f32), pltpu.VMEM((W, HALF), f32), vec,
            vec, pltpu.VMEM((CAP + 8, W), f32), pltpu.VMEM((CAP + 8, W), f32),
            vec, vec, vec, vec, vec,
            dma((4,)), dma((2,)), dma((3,)), dma((3,)), dma((3,)), dma((3,)), dma((2,)), dma((2,)),
            dma((2,)), dma((2,)), dma((2, 3)), dma((2, 3)), dma((2, 3)), dma((2, 3)),
        ],
        compiler_params=pltpu.CompilerParams(
            collective_id=0, has_side_effects=True, vmem_limit_bytes=58 * 1024 * 1024
        ),
        name="solve",
    )(seg, links, rhs[0], diag[0], low[0], coup[0], pre[0])
    return sol[None], res[None]


def solution(mesh):
    in_specs = (
        P("strip", "track", None),
        P("strip", "track", None, None),
        P("strip", "track", None, None),
        P("strip", "track", None, None),
        P("strip", "track", None, None),
        P("track"),
        P("strip", "track"),
    )
    out_specs = (P("strip", "track", None), P("strip", "track", None))
    return jax.shard_map(body, mesh=mesh, in_specs=in_specs, out_specs=out_specs, check_vma=False)
```

```python
import jax
import jax.numpy as jnp
from jax import lax
from jax.experimental import pallas as pl
from jax.experimental.pallas import tpu as pltpu
from jax.sharding import PartitionSpec as P

ITERS = 6
CAP = 16
W = 256
HALF = 128
NX, NY, NS = 4, 4, 4
NT = 32
MESH = pl.DeviceIdType.MESH
f32, bf16 = jnp.float32, jnp.bfloat16


def split2(x):
    hi = x.astype(bf16)
    return hi, (x - hi.astype(f32)).astype(bf16)


def split3(x):
    hi = x.astype(bf16)
    rest = x - hi.astype(f32)
    mid = rest.astype(bf16)
    lo = (rest - mid.astype(f32)).astype(bf16)
    return jnp.concatenate([hi, mid, lo], axis=0)


def dot(a, b):
    return jnp.dot(a, b, preferred_element_type=f32)


def dot_nt(a, b):
    return lax.dot_general(a, b, (((1,), (1,)), ((), ())), preferred_element_type=f32)


def mm(a, b):
    ah, al = split2(a)
    bh, bl = split2(b)
    return dot(ah, bh) + (dot(al, bh) + dot(ah, bl))


def fold(acc):
    return acc[0:16] + acc[16:32] + acc[32:48]


def flip(mat):
    return dot_nt(eye().astype(bf16), mat).astype(bf16)


def eye():
    rows = lax.broadcasted_iota(jnp.int32, (W, W), 0)
    cols = lax.broadcasted_iota(jnp.int32, (W, W), 1)
    return jnp.where(rows == cols, 1.0, 0.0).astype(f32)


def kernel(
    seg, links, rhs, diag_h, low_h, coup_h, pre_h, sol_out, res_out,
    diag, low, coup, pre, low_t, coup_t,
    steps, prefix, ends, scans, tails,
    own, other, chip, xm, row, ym, work,
    hot, msg, got, smsg, sgot, up_buf, up_got, down_buf, down_got, edge_buf, edge_got,
    group, column, car, loc, prevs, shifts, x_s, r_s, z_s, w_s, q_s,
    load_sem, pair_sem, sx_sem, rx_sem, sf_sem, rf_sem, sy_sem, ry_sem,
    gs_sem, gr_sem, ss_sem, sr_sem, hs_sem, hr_sem,
):
    t = lax.axis_index("track")
    s = lax.axis_index("strip")
    core = lax.rem(t, 2)
    x = lax.rem(t // 2, NX)
    y = t // (2 * NX)
    mate = t + 1 - 2 * core

    quarter = lambda ref, g: ref.at[pl.ds(4 * g, 4)]
    loads = []
    for g in range(4):
        for n, (src, dst) in enumerate(((low_h, low), (pre_h, pre))):
            loads.append(
                pltpu.make_async_copy(quarter(src, g), quarter(dst, g), load_sem.at[2 * g + n])
            )
    loads.append(pltpu.make_async_copy(coup_h, coup, load_sem.at[8]))
    loads.append(pltpu.make_async_copy(diag_h, diag, load_sem.at[9]))
    for copy in loads:
        copy.start()

    ym[...] = jnp.zeros_like(ym)
    barrier = pltpu.get_barrier_semaphore()

    def greet(i, _):
        pl.semaphore_signal(
            barrier, inc=1, device_id=(lax.rem(t + i, NT), s), device_id_type=MESH
        )
        return 0

    lax.fori_loop(1, NT, greet, 0)
    for i in range(1, NS):
        pl.semaphore_signal(
            barrier, inc=1, device_id=(t, lax.rem(s + i, NS)), device_id_type=MESH
        )

    count = seg[0]
    slot = lax.broadcasted_iota(jnp.int32, (CAP, W), 0)
    live = jnp.where(slot < count, 1.0, 0.0).astype(f32)
    at_end = jnp.where(slot == count - 1, 1.0, 0.0).astype(f32)
    slots48 = lax.rem(lax.broadcasted_iota(jnp.int32, (48, W), 0), CAP)
    for j in range(CAP):
        hot[j] = jnp.where(slots48 == j, 1.0, 0.0).astype(bf16)
    r_s[...] = rhs[...] * live
    q_s[...] = rhs[...] * live
    for ref in (x_s, z_s, w_s, msg, shifts):
        ref[...] = jnp.zeros_like(ref)


    def make_step(j, _):
        alive = jnp.where(j < count, 1.0, 0.0).astype(f32)
        linked = links[0, j].astype(f32) * alive * jnp.where(j + t > 0, 1.0, 0.0).astype(f32)
        lower = (low[j].astype(f32) * linked).astype(bf16)
        inverse = (pre[j].astype(f32) * alive).astype(bf16)
        lower_t = flip(lower)
        low[j] = lower
        low_t[j] = lower_t
        pre[j] = inverse
        steps[j, 0], steps[j, 1] = split2((1.0 - alive) * eye() - dot_nt(lower_t, inverse))
        return 0

    for g in range(4):
        loads[2 * g].wait()
        loads[2 * g + 1].wait()
        lax.fori_loop(4 * g, 4 * g + 4, make_step, 0, unroll=2)

    for g in range(4):
        prefix[4 * g] = steps[4 * g, 0].astype(f32) + steps[4 * g, 1].astype(f32)

    def make_prefix(n, _):
        for g in range(4):
            j = 4 * g + n
            ah, al = split2(prefix[j - 1])
            bh, bl = steps[j, 0], steps[j, 1]
            prefix[j] = dot(ah, bh) + (dot(al, bh) + dot(ah, bl))
        return 0

    lax.fori_loop(1, 4, make_prefix, 0)
    group[0] = prefix[3]
    group[1] = mm(prefix[3], prefix[7])
    own[...] = mm(group[1], mm(prefix[11], prefix[15]))

    pl.semaphore_wait(barrier, NT - 1 + NS - 1)

    def remote(src, dst, send, recv, tt, ss):
        return pltpu.make_async_remote_copy(
            src_ref=src, dst_ref=dst, send_sem=send, recv_sem=recv,
            device_id=(tt, ss), device_id_type=MESH,
        )

    pair = remote(own, other, pair_sem.at[0], pair_sem.at[1], mate, s)
    pair.start()
    loads[8].wait()
    loads[9].wait()

    group[2] = mm(group[1], prefix[11])

    def join(j, _):
        ah, al = split2(group[j // 4 - 1])
        bh, bl = split2(prefix[j])
        prefix[j] = dot(ah, bh) + (dot(al, bh) + dot(ah, bl))
        return 0

    lax.fori_loop(4, 8, join, 0)
    pair.wait()
    first = core == 0
    chip[...] = mm(
        jnp.where(first, own[...], other[...]), jnp.where(first, other[...], own[...])
    )

    half = pl.ds(pl.multiple_of(core * HALF, HALF), HALF)

    copies = []
    for i in (2, 1, 3):
        to = t + (lax.rem(x + i, NX) - x) * 2
        c = remote(chip.at[half], xm.at[x, half], sx_sem.at[i - 1], rx_sem.at[i - 1], to, s)
        c.start()
        copies.append((i, c))
    xm[x] = chip[...]

    work[...] = eye()

    def make_ends(n, _):
        j = CAP - 1 - n
        alive = jnp.where(j < count, 1.0, 0.0).astype(f32)
        hi, lo = split2(work[...])
        ends[j] = dot(hi, pre[j]) + dot(lo, pre[j])
        bh, bl = split2((1.0 - alive) * eye() - dot(pre[j], low[j]))
        work[...] = dot(hi, bh) + (dot(lo, bh) + dot(hi, bl))
        return 0

    lax.fori_loop(0, CAP, make_ends, 0)

    swaps = []
    for i, c in copies[1:] + copies[:1]:
        c.wait_recv()
        at = lax.rem(x + NX - i, NX)
        c = remote(xm.at[at, half], xm.at[at, half], sf_sem.at[i - 1], rf_sem.at[i - 1], mate, s)
        c.start()
        swaps.append(c)
    lax.fori_loop(8, 12, join, 0)
    for c in swaps:
        c.wait()
    for i, c in copies:
        c.wait_send()

    row[...] = mm(mm(xm[0], xm[1]), mm(xm[2], xm[3]))
    giver = (y == 1) | (y == 2)
    taker = (y == 0) | (y == 3)
    far = jnp.where(y == 1, t - 2 * NX, jnp.where(y == 2, t + 2 * NX, t))
    hop = remote(row.at[half], ym.at[half], sy_sem.at[0], ry_sem.at[0], far, s)

    @pl.when(giver)
    def _():
        hop.start()

    ident = eye()
    one = lambda flag: jnp.where(flag, 1.0, 0.0).astype(f32)
    enter = jnp.where(first, ident, other[...])
    leave = jnp.where(first, other[...], ident)
    work[...] = mm(jnp.where(x > 1, xm[1], ident), jnp.where(x > 2, xm[2], ident))
    scans[2] = (enter * one(x > 0)).T
    behind = xm[lax.rem(x + 3, NX)]
    scans[3] = (mm(behind, enter) * one(x > 1)).T
    scans[4] = (mm(mm(xm[lax.rem(x + 2, NX)], behind), enter) * one(x > 2)).T
    scans[5] = ident * one(core > 0)
    work[...] = mm(mm(jnp.where(x > 0, xm[0], ident), work[...]), enter)
    scans[0] = (work[...] * one(y > 0)).T
    tails[0] = ident
    tails[1] = leave
    chip[...] = mm(
        mm(jnp.where(x < 1, xm[1], ident), jnp.where(x < 2, xm[2], ident)),
        jnp.where(x < 3, xm[3], ident),
    )
    own[...] = mm(leave, chip[...])
    tails[2] = own[...]
    lax.fori_loop(12, CAP, join, 0)

    def flip_coup(j, _):
        coup_t[j] = flip(coup[j])
        return 0

    lax.fori_loop(0, CAP, flip_coup, 0, unroll=2)
    hi, lo = split2(prefix[0])
    tails[4] = dot(hi, low[0]) + dot(lo, low[0])

    @pl.when(giver)
    def _():
        hop.wait_send()

    @pl.when(taker)
    def _():
        hop.wait_recv()
        c = remote(ym.at[half], ym.at[half], sy_sem.at[1], ry_sem.at[1], mate, s)
        c.start()
        c.wait()

    over = mm(jnp.where(y == 0, own[...], ym[...]), jnp.where(y == 0, ym[...], work[...]))
    scans[1] = (over * one(y == 3)).T
    tails[3] = jnp.where(y == 0, over, own[...])

    def each_slot(vec, mats, form=dot):
        parts = split3(vec)
        acc = jnp.zeros((48, W), f32)
        for j in range(CAP):
            acc = acc + form(parts * hot[j], mats[j])
        return acc

    def to_column(vecs, mats):
        for b in range(0, W, 8):
            left = right = None
            for i, (v0, v1) in enumerate(vecs):
                p0 = mats[i, b : b + 8, :HALF] * v0
                p1 = mats[i, b : b + 8, HALF:] * v1
                left = p0 if left is None else left + p0
                right = p1 if right is None else right + p1
            total = jnp.sum(left + right, axis=1, keepdims=True)
            column[b : b + 8] = jnp.broadcast_to(total, (8, HALF))

    def to_row(mats, j):
        left = right = None
        for b in range(0, W, 8):
            part = column[b : b + 8]
            p0 = part * mats[j, b : b + 8, :HALF]
            p1 = part * mats[j, b : b + 8, HALF:]
            left = p0 if left is None else left + p0
            right = p1 if right is None else right + p1
        return jnp.sum(left, axis=0, keepdims=True), jnp.sum(right, axis=0, keepdims=True)

    wide = lambda row: jnp.broadcast_to(row, (8, HALF))

    hops = lambda d: min(d, 4 - d)
    places = [(dy, dx, dc) for dy in range(NY) for dx in range(NX) for dc in range(2)][1:]
    places.sort(key=lambda p: -(2 * (hops(p[0]) + hops(p[1])) + p[2]))
    routes = []
    for dy, dx, dc in places:
        to = lax.rem(y + dy, NY) * 2 * NX + lax.rem(x + dx, NX) * 2 + lax.rem(core + dc, 2)
        kind = 3 if dy > 1 else 2 if dy else 1 if dx else 0
        at = (-dy % NY) * 2 * NX + (-dx % NX) * 2 + dc - 1
        routes.append((to, kind, at))

    def exchange_start(par):
        for to, kind, at in routes:
            remote(
                msg.at[par, kind], got.at[par, at], gs_sem.at[par], gr_sem.at[par], to, s
            ).start()

    def exchange_end(par):
        whole = got.at[par]
        pltpu.make_async_copy(whole, whole, gr_sem.at[par]).wait()
        pltpu.make_async_copy(whole, whole, gs_sem.at[par]).wait()

    def class_sums(par):
        rows = []
        for d in range(1, NY):
            first_at = (NY - d) * 2 * NX - 1
            total = got[par, first_at]
            for i in range(1, 2 * NX):
                total = total + got[par, first_at + i]
            rows.append(total)
        cols = [
            got[par, (NX - d) * 2 - 1] + got[par, (NX - d) * 2] for d in range(1, NX)
        ]
        return rows, cols, got[par, 0]

    def strips_start(par, rows, cols, near):
        total = msg[par, 0] + near
        for part in rows + cols:
            total = total + part
        smsg[par] = total
        out = []
        for i in range(1, NS):
            c = remote(
                smsg.at[par], sgot.at[par, i - 1], ss_sem.at[par, i - 1], sr_sem.at[par, i - 1],
                t, lax.rem(s + i, NS),
            )
            c.start()
            out.append(c)
        return out

    def strips_end(par, out):
        for c in out:
            c.wait()
        total = smsg[par] + sgot[par, 0] + sgot[par, 1] + sgot[par, 2]
        inner = jnp.sum(total[2:3], axis=1, keepdims=True)
        energy = jnp.sum(total[3:4], axis=1, keepdims=True)
        return inner / (energy + 1e-6)

    def put_sums(par):
        prod = r_s[...] * w_s[...]
        square = w_s[...] * w_s[...]
        prod = jnp.sum(prod, axis=0, keepdims=True)
        square = jnp.sum(square, axis=0, keepdims=True)
        prod = prod[:, :HALF] + prod[:, HALF:]
        square = square[:, :HALF] + square[:, HALF:]
        for kind in range(4):
            msg[par, kind, 2:3] = prod
            msg[par, kind, 3:4] = square

    def iteration(k, _):
        par = lax.rem(k, 2)
        put_sums(par)
        vec = q_s[...]
        to_column(
            [(wide(q_s[i : i + 1, :HALF]), wide(q_s[i : i + 1, HALF:])) for i in range(CAP)], ends
        )
        for kind in range(4):
            msg[par, kind, 0:1], msg[par, kind, 1:2] = to_row(tails, kind)
        exchange_start(par)

        loc[...] = fold(each_slot(vec, pre, dot_nt))
        prev = loc[0:1]
        for j in range(1, CAP):
            parts = split3(prev)
            out = dot(parts, steps[j, 0]) + dot(parts, steps[j, 1])
            prev = loc[j : j + 1] + jnp.sum(out, axis=0, keepdims=True)
            loc[j : j + 1] = prev

        edge_loc = jnp.sum(dot(split3(loc[...]) * hot[0], low[0]), axis=0, keepdims=True)
        edge_buf[par] = edge_loc

        exchange_end(par)
        rows, cols, near = class_sums(par)
        sums = strips_start(par, rows, cols, near)
        heads = [rows[0] + rows[1] * one(y == 2), rows[1] + rows[2]] + cols + [near]
        to_column([(wide(h[0:1]), wide(h[1:2])) for h in heads], scans)
        for j in range(CAP):
            car[j : j + 1, :HALF], car[j : j + 1, HALF:] = to_row(prefix, j)
        step = (loc[...] + car[...]) * live
        up_buf[par] = step
        up = remote(
            up_buf.at[par], up_got.at[par], hs_sem.at[par, 0], hr_sem.at[par, 0],
            t, lax.rem(s + 1, NS),
        )
        up.start()
        left, right = to_row(tails, 4)
        edge_buf[par, :, :HALF] = edge_buf[par, :, :HALF] + left
        edge_buf[par, :, HALF:] = edge_buf[par, :, HALF:] + right
        edge = remote(
            edge_buf.at[par], edge_got.at[par], hs_sem.at[par, 1], hr_sem.at[par, 1],
            lax.rem(t + NT - 1, NT), s,
        )
        edge.start()
        down_buf[par] = fold(each_slot(step, coup))
        down = remote(
            down_buf.at[par], down_got.at[par], hs_sem.at[par, 2], hr_sem.at[par, 2],
            t, lax.rem(s + NS - 1, NS),
        )
        down.start()
        prevs[0:1, :HALF], prevs[0:1, HALF:] = to_row(tails, 0)
        shifts[0:CAP] = fold(each_slot(step, low))
        prevs[1 : CAP + 1] = step
        total = fold(each_slot(step, diag, dot_nt) + each_slot(prevs[0:CAP], low_t)) + shifts[1 : CAP + 1]
        alpha = strips_end(par, sums)
        alpha = jnp.broadcast_to(alpha, (CAP, W))
        start = k == 0
        r_s[...] = r_s[...] - jnp.where(start, 0.0, alpha * w_s[...])
        x_s[...] = x_s[...] + jnp.where(start, 0.0, alpha * z_s[...])
        z_s[...] = jnp.where(start, step, z_s[...] - alpha * step)
        up.wait()
        zero = jnp.zeros((CAP, W), f32)
        below = jnp.where(s > 0, up_got[par], zero)
        total = total + fold(each_slot(below, coup_t))
        edge.wait()
        down.wait()
        total = total + jnp.where(s < NS - 1, down_got[par], zero)
        nxt = jnp.broadcast_to(edge_got[par], (CAP, W))
        total = (total + at_end * jnp.where(t < NT - 1, nxt, zero)) * live
        image = jnp.where(start, total, w_s[...] - alpha * total)
        w_s[...] = image
        q_s[...] = image
        return 0

    lax.fori_loop(0, ITERS, iteration, 0)
    par = ITERS % 2
    put_sums(par)
    exchange_start(par)
    exchange_end(par)
    alpha = jnp.broadcast_to(strips_end(par, strips_start(par, *class_sums(par))), (CAP, W))
    sol_out[...] = x_s[...] + alpha * z_s[...]
    res_out[...] = r_s[...] - alpha * w_s[...]


def body(rhs, diag, low, coup, pre, seg, links):
    vmem = pl.BlockSpec(memory_space=pltpu.VMEM)
    smem = pl.BlockSpec(memory_space=pltpu.SMEM)
    anyw = pl.BlockSpec(memory_space=pl.ANY)
    mats = pltpu.VMEM((CAP, W, W), bf16)
    mats2 = pltpu.VMEM((CAP, 2, W, W), bf16)
    big = pltpu.VMEM((W, W), f32)
    big4 = pltpu.VMEM((4, W, W), f32)
    vec = pltpu.VMEM((CAP, W), f32)
    dma = pltpu.SemaphoreType.DMA
    out = jax.ShapeDtypeStruct((CAP, W), f32)
    sol, res = pl.pallas_call(
        kernel,
        out_shape=(out, out),
        in_specs=[smem, smem, vmem, anyw, anyw, anyw, anyw],
        out_specs=(vmem, vmem),
        scratch_shapes=[mats] * 6
        + [
            mats2, pltpu.VMEM((CAP, W, W), f32), pltpu.VMEM((CAP, W, W), f32),
            pltpu.VMEM((6, W, W), f32), pltpu.VMEM((5, W, W), f32),
            big, big, big, big4, big, big, big,
            pltpu.VMEM((CAP, 48, W), bf16),
            pltpu.VMEM((2, 4, 4, HALF), f32), pltpu.VMEM((2, NT - 1, 4, HALF), f32),
            pltpu.VMEM((2, 4, HALF), f32), pltpu.VMEM((2, NS - 1, 4, HALF), f32),
            pltpu.VMEM((2, CAP, W), f32), pltpu.VMEM((2, CAP, W), f32),
            pltpu.VMEM((2, CAP, W), f32), pltpu.VMEM((2, CAP, W), f32),
            pltpu.VMEM((2, 1, W), f32), pltpu.VMEM((2, 1, W), f32),
            pltpu.VMEM((3, W, W), f32), pltpu.VMEM((W, HALF), f32), vec,
            vec, pltpu.VMEM((CAP + 8, W), f32), pltpu.VMEM((CAP + 8, W), f32),
            vec, vec, vec, vec, vec,
            dma((10,)), dma((2,)), dma((3,)), dma((3,)), dma((3,)), dma((3,)), dma((2,)), dma((2,)),
            dma((2,)), dma((2,)), dma((2, 3)), dma((2, 3)), dma((2, 3)), dma((2, 3)),
        ],
        compiler_params=pltpu.CompilerParams(
            collective_id=0, has_side_effects=True, vmem_limit_bytes=58 * 1024 * 1024
        ),
        name="solve",
    )(seg, links, rhs[0], diag[0], low[0], coup[0], pre[0])
    return sol[None], res[None]


def solution(mesh):
    in_specs = (
        P("strip", "track", None),
        P("strip", "track", None, None),
        P("strip", "track", None, None),
        P("strip", "track", None, None),
        P("strip", "track", None, None),
        P("track"),
        P("strip", "track"),
    )
    out_specs = (P("strip", "track", None), P("strip", "track", None))
    return jax.shard_map(body, mesh=mesh, in_specs=in_specs, out_specs=out_specs, check_vma=False)
```

```python
import jax
import jax.numpy as jnp
from jax import lax
from jax.experimental import pallas as pl
from jax.experimental.pallas import tpu as pltpu
from jax.sharding import PartitionSpec as P

ITERS = 6
CAP = 16
W = 256
HALF = 128
NX, NY, NS = 4, 4, 4
NT = 32
MESH = pl.DeviceIdType.MESH
f32, bf16 = jnp.float32, jnp.bfloat16


def split2(x):
    hi = x.astype(bf16)
    return hi, (x - hi.astype(f32)).astype(bf16)


def split3(x):
    hi = x.astype(bf16)
    rest = x - hi.astype(f32)
    mid = rest.astype(bf16)
    lo = (rest - mid.astype(f32)).astype(bf16)
    return jnp.concatenate([hi, mid, lo], axis=0)


def dot(a, b):
    return jnp.dot(a, b, preferred_element_type=f32)


def dot_nt(a, b):
    return lax.dot_general(a, b, (((1,), (1,)), ((), ())), preferred_element_type=f32)


def mm(a, b):
    ah, al = split2(a)
    bh, bl = split2(b)
    return dot(ah, bh) + (dot(al, bh) + dot(ah, bl))


def fold(acc):
    return acc[0:16] + acc[16:32] + acc[32:48]


def flip(mat):
    return dot_nt(eye().astype(bf16), mat).astype(bf16)


def eye():
    rows = lax.broadcasted_iota(jnp.int32, (W, W), 0)
    cols = lax.broadcasted_iota(jnp.int32, (W, W), 1)
    return jnp.where(rows == cols, 1.0, 0.0).astype(f32)


def kernel(
    seg, links, rhs, diag_h, low_h, coup_h, pre_h, state_h, alpha_out,
    diag, low, coup, pre, low_t, coup_t,
    steps, prefix, ends, scans, tails,
    own, other, chip, xm, row, ym, work, work2,
    hot, msg, got, smsg, sgot, up_buf, up_got, down_buf, down_got, edge_buf, edge_got,
    group, column, car, loc, prevs, shifts, x_s, r_s, z_s, w_s, q_s,
    load_sem, pair_sem, sx_sem, rx_sem, sf_sem, rf_sem, sy_sem, ry_sem,
    gs_sem, gr_sem, ss_sem, sr_sem, hs_sem, hr_sem,
):
    t = lax.axis_index("track")
    s = lax.axis_index("strip")
    core = lax.rem(t, 2)
    x = lax.rem(t // 2, NX)
    y = t // (2 * NX)
    mate = t + 1 - 2 * core

    quarter = lambda ref, g: ref.at[pl.ds(4 * g, 4)]
    loads = []
    for g in range(4):
        for n, (src, dst) in enumerate(((low_h, low), (pre_h, pre))):
            loads.append(
                pltpu.make_async_copy(quarter(src, g), quarter(dst, g), load_sem.at[2 * g + n])
            )
    loads.append(pltpu.make_async_copy(coup_h, coup, load_sem.at[8]))
    loads.append(pltpu.make_async_copy(diag_h, diag, load_sem.at[9]))
    for copy in loads:
        copy.start()

    ym[...] = jnp.zeros_like(ym)
    barrier = pltpu.get_barrier_semaphore()

    def greet(i, _):
        pl.semaphore_signal(
            barrier, inc=1, device_id=(lax.rem(t + i, NT), s), device_id_type=MESH
        )
        return 0

    lax.fori_loop(1, NT, greet, 0)
    for i in range(1, NS):
        pl.semaphore_signal(
            barrier, inc=1, device_id=(t, lax.rem(s + i, NS)), device_id_type=MESH
        )

    count = seg[0]
    slot = lax.broadcasted_iota(jnp.int32, (CAP, W), 0)
    live = jnp.where(slot < count, 1.0, 0.0).astype(f32)
    at_end = jnp.where(slot == count - 1, 1.0, 0.0).astype(f32)
    slots48 = lax.rem(lax.broadcasted_iota(jnp.int32, (48, W), 0), CAP)
    for j in range(CAP):
        hot[j] = jnp.where(slots48 == j, 1.0, 0.0).astype(bf16)
    r_s[...] = rhs[...] * live
    q_s[...] = rhs[...] * live
    for ref in (x_s, z_s, w_s, msg, shifts):
        ref[...] = jnp.zeros_like(ref)


    def make_step(j, _):
        alive = jnp.where(j < count, 1.0, 0.0).astype(f32)
        linked = links[0, j].astype(f32) * alive * jnp.where(j + t > 0, 1.0, 0.0).astype(f32)
        lower = (low[j].astype(f32) * linked).astype(bf16)
        inverse = (pre[j].astype(f32) * alive).astype(bf16)
        lower_t = flip(lower)
        low[j] = lower
        low_t[j] = lower_t
        pre[j] = inverse
        steps[j, 0], steps[j, 1] = split2((1.0 - alive) * eye() - dot_nt(lower_t, inverse))
        return 0

    for g in range(4):
        loads[2 * g].wait()
        loads[2 * g + 1].wait()
        lax.fori_loop(4 * g, 4 * g + 4, make_step, 0, unroll=2)

    for g in range(4):
        prefix[4 * g] = steps[4 * g, 0].astype(f32) + steps[4 * g, 1].astype(f32)

    def make_prefix(n, _):
        for g in range(4):
            j = 4 * g + n
            ah, al = split2(prefix[j - 1])
            bh, bl = steps[j, 0], steps[j, 1]
            prefix[j] = dot(ah, bh) + (dot(al, bh) + dot(ah, bl))
        return 0

    lax.fori_loop(1, 4, make_prefix, 0)
    group[0] = prefix[3]
    group[1] = mm(prefix[3], prefix[7])
    own[...] = mm(group[1], mm(prefix[11], prefix[15]))

    pl.semaphore_wait(barrier, NT - 1 + NS - 1)

    def remote(src, dst, send, recv, tt, ss):
        return pltpu.make_async_remote_copy(
            src_ref=src, dst_ref=dst, send_sem=send, recv_sem=recv,
            device_id=(tt, ss), device_id_type=MESH,
        )

    pair = remote(own, other, pair_sem.at[0], pair_sem.at[1], mate, s)
    pair.start()
    loads[8].wait()
    loads[9].wait()

    group[2] = mm(group[1], prefix[11])

    def join(j, _):
        ah, al = split2(group[j // 4 - 1])
        bh, bl = split2(prefix[j])
        prefix[j] = dot(ah, bh) + (dot(al, bh) + dot(ah, bl))
        return 0

    lax.fori_loop(4, 8, join, 0)
    pair.wait()
    first = core == 0
    chip[...] = mm(
        jnp.where(first, own[...], other[...]), jnp.where(first, other[...], own[...])
    )

    half = pl.ds(pl.multiple_of(core * HALF, HALF), HALF)

    copies = []
    for i in (2, 1, 3):
        to = t + (lax.rem(x + i, NX) - x) * 2
        c = remote(chip.at[half], xm.at[x, half], sx_sem.at[i - 1], rx_sem.at[i - 1], to, s)
        c.start()
        copies.append((i, c))
    xm[x] = chip[...]

    work[...] = eye()
    work2[...] = eye()

    def make_ends(n, _):
        for j, ref in ((CAP - 1 - n, work), (CAP // 2 - 1 - n, work2)):
            alive = jnp.where(j < count, 1.0, 0.0).astype(f32)
            hi, lo = split2(ref[...])
            ends[j] = dot(hi, pre[j]) + dot(lo, pre[j])
            bh, bl = split2((1.0 - alive) * eye() - dot(pre[j], low[j]))
            ref[...] = dot(hi, bh) + (dot(lo, bh) + dot(hi, bl))
        return 0

    lax.fori_loop(0, CAP // 2, make_ends, 0)
    lax.fori_loop(8, 12, join, 0)

    swaps = []
    for i, c in copies[1:] + copies[:1]:
        c.wait_recv()
        at = lax.rem(x + NX - i, NX)
        c = remote(xm.at[at, half], xm.at[at, half], sf_sem.at[i - 1], rf_sem.at[i - 1], mate, s)
        c.start()
        swaps.append(c)

    def carry_ends(j, _):
        ends[j] = mm(work[...], ends[j])
        return 0

    lax.fori_loop(0, CAP // 2, carry_ends, 0)
    for c in swaps:
        c.wait()
    for i, c in copies:
        c.wait_send()

    row[...] = mm(mm(xm[0], xm[1]), mm(xm[2], xm[3]))
    giver = (y == 1) | (y == 2)
    taker = (y == 0) | (y == 3)
    far = jnp.where(y == 1, t - 2 * NX, jnp.where(y == 2, t + 2 * NX, t))
    hop = remote(row.at[half], ym.at[half], sy_sem.at[0], ry_sem.at[0], far, s)

    @pl.when(giver)
    def _():
        hop.start()

    ident = eye()
    one = lambda flag: jnp.where(flag, 1.0, 0.0).astype(f32)
    enter = jnp.where(first, ident, other[...])
    leave = jnp.where(first, other[...], ident)
    work[...] = mm(jnp.where(x > 1, xm[1], ident), jnp.where(x > 2, xm[2], ident))
    scans[2] = (enter * one(x > 0)).T
    behind = xm[lax.rem(x + 3, NX)]
    scans[3] = (mm(behind, enter) * one(x > 1)).T
    scans[4] = (mm(mm(xm[lax.rem(x + 2, NX)], behind), enter) * one(x > 2)).T
    scans[5] = ident * one(core > 0)
    work[...] = mm(mm(jnp.where(x > 0, xm[0], ident), work[...]), enter)
    scans[0] = (work[...] * one(y > 0)).T
    tails[0] = ident
    tails[1] = leave
    chip[...] = mm(
        mm(jnp.where(x < 1, xm[1], ident), jnp.where(x < 2, xm[2], ident)),
        jnp.where(x < 3, xm[3], ident),
    )
    own[...] = mm(leave, chip[...])
    tails[2] = own[...]
    lax.fori_loop(12, CAP, join, 0)

    def flip_coup(j, _):
        coup_t[j] = flip(coup[j])
        return 0

    lax.fori_loop(0, CAP, flip_coup, 0, unroll=2)
    hi, lo = split2(prefix[0])
    tails[4] = dot(hi, low[0]) + dot(lo, low[0])

    @pl.when(giver)
    def _():
        hop.wait_send()

    @pl.when(taker)
    def _():
        hop.wait_recv()
        c = remote(ym.at[half], ym.at[half], sy_sem.at[1], ry_sem.at[1], mate, s)
        c.start()
        c.wait()

    over = mm(jnp.where(y == 0, own[...], ym[...]), jnp.where(y == 0, ym[...], work[...]))
    scans[1] = (over * one(y == 3)).T
    tails[3] = jnp.where(y == 0, over, own[...])

    def each_slot(vec, mats, form=dot):
        parts = split3(vec)
        acc = jnp.zeros((48, W), f32)
        for j in range(CAP):
            acc = acc + form(parts * hot[j], mats[j])
        return acc

    def to_column(vecs, mats):
        for b in range(0, W, 8):
            left = right = None
            for i, (v0, v1) in enumerate(vecs):
                p0 = mats[i, b : b + 8, :HALF] * v0
                p1 = mats[i, b : b + 8, HALF:] * v1
                left = p0 if left is None else left + p0
                right = p1 if right is None else right + p1
            total = jnp.sum(left + right, axis=1, keepdims=True)
            column[b : b + 8] = jnp.broadcast_to(total, (8, HALF))

    def to_row(mats, j):
        left = right = None
        for b in range(0, W, 8):
            part = column[b : b + 8]
            p0 = part * mats[j, b : b + 8, :HALF]
            p1 = part * mats[j, b : b + 8, HALF:]
            left = p0 if left is None else left + p0
            right = p1 if right is None else right + p1
        return jnp.sum(left, axis=0, keepdims=True), jnp.sum(right, axis=0, keepdims=True)

    wide = lambda row: jnp.broadcast_to(row, (8, HALF))

    hops = lambda d: min(d, 4 - d)
    places = [(dy, dx, dc) for dy in range(NY) for dx in range(NX) for dc in range(2)][1:]
    places.sort(key=lambda p: -(2 * (hops(p[0]) + hops(p[1])) + p[2]))
    routes = []
    for dy, dx, dc in places:
        to = lax.rem(y + dy, NY) * 2 * NX + lax.rem(x + dx, NX) * 2 + lax.rem(core + dc, 2)
        kind = 3 if dy > 1 else 2 if dy else 1 if dx else 0
        at = (-dy % NY) * 2 * NX + (-dx % NX) * 2 + dc - 1
        routes.append((to, kind, at))

    def exchange_start(par):
        for to, kind, at in routes:
            remote(
                msg.at[par, kind], got.at[par, at], gs_sem.at[par], gr_sem.at[par], to, s
            ).start()

    def exchange_end(par):
        whole = got.at[par]
        pltpu.make_async_copy(whole, whole, gr_sem.at[par]).wait()

    def send_end(par):
        whole = got.at[par]
        pltpu.make_async_copy(whole, whole, gs_sem.at[par]).wait()

    def class_sums(par):
        rows = []
        for d in range(1, NY):
            first_at = (NY - d) * 2 * NX - 1
            total = got[par, first_at]
            for i in range(1, 2 * NX):
                total = total + got[par, first_at + i]
            rows.append(total)
        cols = [
            got[par, (NX - d) * 2 - 1] + got[par, (NX - d) * 2] for d in range(1, NX)
        ]
        return rows, cols, got[par, 0]

    def strips_start(par, rows, cols, near):
        total = msg[par, 0] + near
        for part in rows + cols:
            total = total + part
        smsg[par] = total
        out = []
        for i in range(1, NS):
            c = remote(
                smsg.at[par], sgot.at[par, i - 1], ss_sem.at[par, i - 1], sr_sem.at[par, i - 1],
                t, lax.rem(s + i, NS),
            )
            c.start()
            out.append(c)
        return out

    def strips_end(par, out):
        for c in out:
            c.wait()
        total = smsg[par] + sgot[par, 0] + sgot[par, 1] + sgot[par, 2]
        inner = jnp.sum(total[2:3], axis=1, keepdims=True)
        energy = jnp.sum(total[3:4], axis=1, keepdims=True)
        return inner / (energy + 1e-6)

    def put_sums(par):
        prod = r_s[...] * w_s[...]
        square = w_s[...] * w_s[...]
        prod = jnp.sum(prod, axis=0, keepdims=True)
        square = jnp.sum(square, axis=0, keepdims=True)
        prod = prod[:, :HALF] + prod[:, HALF:]
        square = square[:, :HALF] + square[:, HALF:]
        for kind in range(4):
            msg[par, kind, 2:3] = prod
            msg[par, kind, 3:4] = square

    def iteration(k, _):
        par = lax.rem(k, 2)
        put_sums(par)
        vec = q_s[...]
        to_column(
            [(wide(q_s[i : i + 1, :HALF]), wide(q_s[i : i + 1, HALF:])) for i in range(CAP)], ends
        )
        for kind in range(4):
            msg[par, kind, 0:1], msg[par, kind, 1:2] = to_row(tails, kind)
        exchange_start(par)

        loc[...] = fold(each_slot(vec, pre, dot_nt))
        prev = loc[0:1]
        for j in range(1, CAP):
            parts = split3(prev)
            out = dot(parts, steps[j, 0]) + dot(parts, steps[j, 1])
            prev = loc[j : j + 1] + jnp.sum(out, axis=0, keepdims=True)
            loc[j : j + 1] = prev

        edge_loc = jnp.sum(dot(split3(loc[...]) * hot[0], low[0]), axis=0, keepdims=True)
        edge_buf[par] = edge_loc

        exchange_end(par)
        rows, cols, near = class_sums(par)
        sums = strips_start(par, rows, cols, near)
        heads = [rows[0] + rows[1] * one(y == 2), rows[1] + rows[2]] + cols + [near]
        to_column([(wide(h[0:1]), wide(h[1:2])) for h in heads], scans)
        for j in range(CAP):
            car[j : j + 1, :HALF], car[j : j + 1, HALF:] = to_row(prefix, j)
        step = (loc[...] + car[...]) * live
        up_buf[par] = step
        up = remote(
            up_buf.at[par], up_got.at[par], hs_sem.at[par, 0], hr_sem.at[par, 0],
            t, lax.rem(s + 1, NS),
        )
        up.start()
        left, right = to_row(tails, 4)
        edge_buf[par, :, :HALF] = edge_buf[par, :, :HALF] + left
        edge_buf[par, :, HALF:] = edge_buf[par, :, HALF:] + right
        edge = remote(
            edge_buf.at[par], edge_got.at[par], hs_sem.at[par, 1], hr_sem.at[par, 1],
            lax.rem(t + NT - 1, NT), s,
        )
        edge.start()
        down_buf[par] = fold(each_slot(step, coup))
        down = remote(
            down_buf.at[par], down_got.at[par], hs_sem.at[par, 2], hr_sem.at[par, 2],
            t, lax.rem(s + NS - 1, NS),
        )
        down.start()
        prevs[0:1, :HALF], prevs[0:1, HALF:] = to_row(tails, 0)
        shifts[0:CAP] = fold(each_slot(step, low))
        prevs[1 : CAP + 1] = step
        total = fold(each_slot(step, diag, dot_nt) + each_slot(prevs[0:CAP], low_t)) + shifts[1 : CAP + 1]
        alpha = strips_end(par, sums)
        alpha = jnp.broadcast_to(alpha, (CAP, W))
        start = k == 0
        r_s[...] = r_s[...] - jnp.where(start, 0.0, alpha * w_s[...])
        x_s[...] = x_s[...] + jnp.where(start, 0.0, alpha * z_s[...])
        z_s[...] = jnp.where(start, step, z_s[...] - alpha * step)
        up.wait_recv()
        zero = jnp.zeros((CAP, W), f32)
        below = jnp.where(s > 0, up_got[par], zero)
        total = total + fold(each_slot(below, coup_t))
        edge.wait_recv()
        down.wait_recv()
        total = total + jnp.where(s < NS - 1, down_got[par], zero)
        nxt = jnp.broadcast_to(edge_got[par], (CAP, W))
        total = (total + at_end * jnp.where(t < NT - 1, nxt, zero)) * live
        image = jnp.where(start, total, w_s[...] - alpha * total)
        w_s[...] = image
        q_s[...] = image
        for c in (up, edge, down):
            c.wait_send()
        send_end(par)
        return 0

    lax.fori_loop(0, ITERS, iteration, 0)
    par = ITERS % 2
    put_sums(par)
    exchange_start(par)
    leaving = []
    for n, ref in enumerate((x_s, z_s, r_s, w_s)):
        c = pltpu.make_async_copy(ref, state_h.at[n], load_sem.at[n])
        c.start()
        leaving.append(c)
    exchange_end(par)
    alpha_out[...] = jnp.broadcast_to(strips_end(par, strips_start(par, *class_sums(par))), (CAP, W))
    send_end(par)
    for c in leaving:
        c.wait()


def body(rhs, diag, low, coup, pre, seg, links):
    vmem = pl.BlockSpec(memory_space=pltpu.VMEM)
    smem = pl.BlockSpec(memory_space=pltpu.SMEM)
    anyw = pl.BlockSpec(memory_space=pl.ANY)
    mats = pltpu.VMEM((CAP, W, W), bf16)
    mats2 = pltpu.VMEM((CAP, 2, W, W), bf16)
    big = pltpu.VMEM((W, W), f32)
    big4 = pltpu.VMEM((4, W, W), f32)
    vec = pltpu.VMEM((CAP, W), f32)
    dma = pltpu.SemaphoreType.DMA
    out = jax.ShapeDtypeStruct((CAP, W), f32)
    state, alpha = pl.pallas_call(
        kernel,
        out_shape=(jax.ShapeDtypeStruct((4, CAP, W), f32), out),
        in_specs=[smem, smem, vmem, anyw, anyw, anyw, anyw],
        out_specs=(anyw, vmem),
        scratch_shapes=[mats] * 6
        + [
            mats2, pltpu.VMEM((CAP, W, W), f32), pltpu.VMEM((CAP, W, W), f32),
            pltpu.VMEM((6, W, W), f32), pltpu.VMEM((5, W, W), f32),
            big, big, big, big4, big, big, big, big,
            pltpu.VMEM((CAP, 48, W), bf16),
            pltpu.VMEM((2, 4, 4, HALF), f32), pltpu.VMEM((2, NT - 1, 4, HALF), f32),
            pltpu.VMEM((2, 4, HALF), f32), pltpu.VMEM((2, NS - 1, 4, HALF), f32),
            pltpu.VMEM((2, CAP, W), f32), pltpu.VMEM((2, CAP, W), f32),
            pltpu.VMEM((2, CAP, W), f32), pltpu.VMEM((2, CAP, W), f32),
            pltpu.VMEM((2, 1, W), f32), pltpu.VMEM((2, 1, W), f32),
            pltpu.VMEM((3, W, W), f32), pltpu.VMEM((W, HALF), f32), vec,
            vec, pltpu.VMEM((CAP + 8, W), f32), pltpu.VMEM((CAP + 8, W), f32),
            vec, vec, vec, vec, vec,
            dma((10,)), dma((2,)), dma((3,)), dma((3,)), dma((3,)), dma((3,)), dma((2,)), dma((2,)),
            dma((2,)), dma((2,)), dma((2, 3)), dma((2, 3)), dma((2, 3)), dma((2, 3)),
        ],
        compiler_params=pltpu.CompilerParams(
            collective_id=0, has_side_effects=True, vmem_limit_bytes=58 * 1024 * 1024
        ),
        name="solve",
    )(seg, links, rhs[0], diag[0], low[0], coup[0], pre[0])
    sol = state[0] + alpha * state[1]
    res = state[2] - alpha * state[3]
    return sol[None], res[None]


def solution(mesh):
    in_specs = (
        P("strip", "track", None),
        P("strip", "track", None, None),
        P("strip", "track", None, None),
        P("strip", "track", None, None),
        P("strip", "track", None, None),
        P("track"),
        P("strip", "track"),
    )
    out_specs = (P("strip", "track", None), P("strip", "track", None))
    return jax.shard_map(body, mesh=mesh, in_specs=in_specs, out_specs=out_specs, check_vma=False)
```

```python
import jax
import jax.numpy as jnp
from jax import lax
from jax.experimental import pallas as pl
from jax.experimental.pallas import tpu as pltpu
from jax.sharding import PartitionSpec as P

ITERS = 6
CAP = 16
W = 256
HALF = 128
NX, NY, NS = 4, 4, 4
NT = 32
MESH = pl.DeviceIdType.MESH
f32, bf16 = jnp.float32, jnp.bfloat16


def split2(x):
    hi = x.astype(bf16)
    return hi, (x - hi.astype(f32)).astype(bf16)


def split3(x):
    hi = x.astype(bf16)
    rest = x - hi.astype(f32)
    mid = rest.astype(bf16)
    lo = (rest - mid.astype(f32)).astype(bf16)
    return jnp.concatenate([hi, mid, lo], axis=0)


def dot(a, b):
    return jnp.dot(a, b, preferred_element_type=f32)


def dot_nt(a, b):
    return lax.dot_general(a, b, (((1,), (1,)), ((), ())), preferred_element_type=f32)


def mm(a, b):
    ah, al = split2(a)
    bh, bl = split2(b)
    return dot(ah, bh) + (dot(al, bh) + dot(ah, bl))


def fold(acc):
    return acc[0:16] + acc[16:32] + acc[32:48]


def flip(mat):
    return dot_nt(eye().astype(bf16), mat).astype(bf16)


def eye():
    rows = lax.broadcasted_iota(jnp.int32, (W, W), 0)
    cols = lax.broadcasted_iota(jnp.int32, (W, W), 1)
    return jnp.where(rows == cols, 1.0, 0.0).astype(f32)


def kernel(
    seg, links, rhs, diag_h, low_h, coup_h, pre_h, state_h, alpha_out,
    diag, low, coup, pre, low_t, coup_t,
    steps, prefix, ends, scans, tails,
    own, other, chip, xm, row, ym, work, work2,
    hot, msg, got, smsg, sgot, up_buf, up_got, down_buf, down_got, edge_buf, edge_got,
    group, column, car, loc, prevs, shifts, x_s, r_s, z_s, w_s, q_s,
    load_sem, pair_sem, sx_sem, rx_sem, sf_sem, rf_sem, sy_sem, ry_sem,
    gs_sem, gr_sem, ss_sem, sr_sem, hs_sem, hr_sem, relay, relay_got, sl_sem, rl_sem,
):
    t = lax.axis_index("track")
    s = lax.axis_index("strip")
    core = lax.rem(t, 2)
    x = lax.rem(t // 2, NX)
    y = t // (2 * NX)
    mate = t + 1 - 2 * core

    quarter = lambda ref, g: ref.at[pl.ds(4 * g, 4)]
    loads = []
    for g in range(4):
        for n, (src, dst) in enumerate(((low_h, low), (pre_h, pre))):
            loads.append(
                pltpu.make_async_copy(quarter(src, g), quarter(dst, g), load_sem.at[2 * g + n])
            )
    loads.append(pltpu.make_async_copy(coup_h, coup, load_sem.at[8]))
    loads.append(pltpu.make_async_copy(diag_h, diag, load_sem.at[9]))
    for copy in loads:
        copy.start()

    ym[...] = jnp.zeros_like(ym)
    relay_got[...] = jnp.zeros_like(relay_got)
    barrier = pltpu.get_barrier_semaphore()

    def greet(i, _):
        pl.semaphore_signal(
            barrier, inc=1, device_id=(lax.rem(t + i, NT), s), device_id_type=MESH
        )
        return 0

    lax.fori_loop(1, NT, greet, 0)
    for i in range(1, NS):
        pl.semaphore_signal(
            barrier, inc=1, device_id=(t, lax.rem(s + i, NS)), device_id_type=MESH
        )

    count = seg[0]
    slot = lax.broadcasted_iota(jnp.int32, (CAP, W), 0)
    live = jnp.where(slot < count, 1.0, 0.0).astype(f32)
    at_end = jnp.where(slot == count - 1, 1.0, 0.0).astype(f32)
    slots48 = lax.rem(lax.broadcasted_iota(jnp.int32, (48, W), 0), CAP)
    for j in range(CAP):
        hot[j] = jnp.where(slots48 == j, 1.0, 0.0).astype(bf16)
    r_s[...] = rhs[...] * live
    q_s[...] = rhs[...] * live
    for ref in (x_s, z_s, w_s, msg, shifts):
        ref[...] = jnp.zeros_like(ref)


    def make_step(j, _):
        alive = jnp.where(j < count, 1.0, 0.0).astype(f32)
        linked = links[0, j].astype(f32) * alive * jnp.where(j + t > 0, 1.0, 0.0).astype(f32)
        lower = (low[j].astype(f32) * linked).astype(bf16)
        inverse = (pre[j].astype(f32) * alive).astype(bf16)
        lower_t = flip(lower)
        low[j] = lower
        low_t[j] = lower_t
        pre[j] = inverse
        steps[j, 0], steps[j, 1] = split2((1.0 - alive) * eye() - dot_nt(lower_t, inverse))
        return 0

    for g in range(4):
        loads[2 * g].wait()
        loads[2 * g + 1].wait()
        lax.fori_loop(4 * g, 4 * g + 4, make_step, 0, unroll=2)

    for g in range(4):
        prefix[4 * g] = steps[4 * g, 0].astype(f32) + steps[4 * g, 1].astype(f32)

    def make_prefix(n, _):
        for g in range(4):
            j = 4 * g + n
            ah, al = split2(prefix[j - 1])
            bh, bl = steps[j, 0], steps[j, 1]
            prefix[j] = dot(ah, bh) + (dot(al, bh) + dot(ah, bl))
        return 0

    lax.fori_loop(1, 4, make_prefix, 0)
    group[0] = prefix[3]
    group[1] = mm(prefix[3], prefix[7])
    own[...] = mm(group[1], mm(prefix[11], prefix[15]))

    pl.semaphore_wait(barrier, NT - 1 + NS - 1)

    def remote(src, dst, send, recv, tt, ss):
        return pltpu.make_async_remote_copy(
            src_ref=src, dst_ref=dst, send_sem=send, recv_sem=recv,
            device_id=(tt, ss), device_id_type=MESH,
        )

    pair = remote(own, other, pair_sem.at[0], pair_sem.at[1], mate, s)
    pair.start()
    loads[8].wait()
    loads[9].wait()

    group[2] = mm(group[1], prefix[11])

    def join(j, _):
        ah, al = split2(group[j // 4 - 1])
        bh, bl = split2(prefix[j])
        prefix[j] = dot(ah, bh) + (dot(al, bh) + dot(ah, bl))
        return 0

    lax.fori_loop(4, 8, join, 0)
    pair.wait()
    first = core == 0
    chip[...] = mm(
        jnp.where(first, own[...], other[...]), jnp.where(first, other[...], own[...])
    )

    half = pl.ds(pl.multiple_of(core * HALF, HALF), HALF)

    copies = []
    for i in (2, 1, 3):
        to = t + (lax.rem(x + i, NX) - x) * 2
        c = remote(chip.at[half], xm.at[x, half], sx_sem.at[i - 1], rx_sem.at[i - 1], to, s)
        c.start()
        copies.append((i, c))
    xm[x] = chip[...]

    work[...] = eye()
    work2[...] = eye()

    def make_ends(n, _):
        for j, ref in ((CAP - 1 - n, work), (CAP // 2 - 1 - n, work2)):
            alive = jnp.where(j < count, 1.0, 0.0).astype(f32)
            hi, lo = split2(ref[...])
            ends[j] = dot(hi, pre[j]) + dot(lo, pre[j])
            bh, bl = split2((1.0 - alive) * eye() - dot(pre[j], low[j]))
            ref[...] = dot(hi, bh) + (dot(lo, bh) + dot(hi, bl))
        return 0

    lax.fori_loop(0, CAP // 2, make_ends, 0)
    lax.fori_loop(8, 12, join, 0)

    swaps = []
    for i, c in copies[1:] + copies[:1]:
        c.wait_recv()
        at = lax.rem(x + NX - i, NX)
        c = remote(xm.at[at, half], xm.at[at, half], sf_sem.at[i - 1], rf_sem.at[i - 1], mate, s)
        c.start()
        swaps.append(c)

    def carry_ends(j, _):
        ends[j] = mm(work[...], ends[j])
        return 0

    lax.fori_loop(0, CAP // 2, carry_ends, 0)
    for c in swaps:
        c.wait()
    for i, c in copies:
        c.wait_send()

    row[...] = mm(mm(xm[0], xm[1]), mm(xm[2], xm[3]))
    giver = (y == 1) | (y == 2)
    taker = (y == 0) | (y == 3)
    far = jnp.where(y == 1, t - 2 * NX, jnp.where(y == 2, t + 2 * NX, t))
    hop = remote(row.at[half], ym.at[half], sy_sem.at[0], ry_sem.at[0], far, s)

    @pl.when(giver)
    def _():
        hop.start()

    ident = eye()
    one = lambda flag: jnp.where(flag, 1.0, 0.0).astype(f32)
    def each_slot(vec, mats, form=dot):
        parts = split3(vec)
        acc = jnp.zeros((48, W), f32)
        for j in range(CAP):
            acc = acc + form(parts * hot[j], mats[j])
        return acc

    def to_column(vecs, mats):
        for b in range(0, W, 8):
            left = right = None
            for i, (v0, v1) in enumerate(vecs):
                p0 = mats[i, b : b + 8, :HALF] * v0
                p1 = mats[i, b : b + 8, HALF:] * v1
                left = p0 if left is None else left + p0
                right = p1 if right is None else right + p1
            total = jnp.sum(left + right, axis=1, keepdims=True)
            column[b : b + 8] = jnp.broadcast_to(total, (8, HALF))

    def to_row(mats, j):
        left = right = None
        for b in range(0, W, 8):
            part = column[b : b + 8]
            p0 = part * mats[j, b : b + 8, :HALF]
            p1 = part * mats[j, b : b + 8, HALF:]
            left = p0 if left is None else left + p0
            right = p1 if right is None else right + p1
        return jnp.sum(left, axis=0, keepdims=True), jnp.sum(right, axis=0, keepdims=True)

    wide = lambda row: jnp.broadcast_to(row, (8, HALF))

    hops = lambda d: min(d, 4 - d)
    places = [(dy, dx, dc) for dy in range(NY) for dx in range(NX) for dc in range(2)][1:]
    places.sort(key=lambda p: -(2 * (hops(p[0]) + hops(p[1])) + p[2]))
    routes = []
    for dy, dx, dc in places:
        to = lax.rem(y + dy, NY) * 2 * NX + lax.rem(x + dx, NX) * 2 + lax.rem(core + dc, 2)
        kind = 3 if dy > 1 else 2 if dy else 1 if dx else 0
        at = (-dy % NY) * 2 * NX + (-dx % NX) * 2 + dc - 1
        routes.append((to, kind, at))

    def exchange_start(par):
        for to, kind, at in routes:
            remote(
                msg.at[par, kind], got.at[par, at], gs_sem.at[par], gr_sem.at[par], to, s
            ).start()

    def exchange_end(par):
        whole = got.at[par]
        pltpu.make_async_copy(whole, whole, gr_sem.at[par]).wait()

    def send_end(par):
        whole = got.at[par]
        pltpu.make_async_copy(whole, whole, gs_sem.at[par]).wait()

    def class_sums(par):
        rows = []
        for d in range(1, NY):
            first_at = (NY - d) * 2 * NX - 1
            total = got[par, first_at]
            for i in range(1, 2 * NX):
                total = total + got[par, first_at + i]
            rows.append(total)
        cols = [
            got[par, (NX - d) * 2 - 1] + got[par, (NX - d) * 2] for d in range(1, NX)
        ]
        return rows, cols, got[par, 0]

    def strips_start(par, rows, cols, near):
        total = msg[par, 0] + near
        for part in rows + cols:
            total = total + part
        smsg[par] = total
        out = []
        for i in range(1, NS):
            c = remote(
                smsg.at[par], sgot.at[par, i - 1], ss_sem.at[par, i - 1], sr_sem.at[par, i - 1],
                t, lax.rem(s + i, NS),
            )
            c.start()
            out.append(c)
        return out

    def strips_end(par, out):
        for c in out:
            c.wait()
        total = smsg[par] + sgot[par, 0] + sgot[par, 1] + sgot[par, 2]
        inner = jnp.sum(total[2:3], axis=1, keepdims=True)
        energy = jnp.sum(total[3:4], axis=1, keepdims=True)
        return inner / (energy + 1e-6)

    def put_sums(par):
        prod = r_s[...] * w_s[...]
        square = w_s[...] * w_s[...]
        prod = jnp.sum(prod, axis=0, keepdims=True)
        square = jnp.sum(square, axis=0, keepdims=True)
        prod = prod[:, :HALF] + prod[:, HALF:]
        square = square[:, :HALF] + square[:, HALF:]
        for kind in range(4):
            msg[par, kind, 2:3] = prod
            msg[par, kind, 3:4] = square

    def make_message(par):
        to_column(
            [(wide(q_s[i : i + 1, :HALF]), wide(q_s[i : i + 1, HALF:])) for i in range(CAP)], ends
        )
        for kind in range(4):
            msg[par, kind, 0:1], msg[par, kind, 1:2] = to_row(tails, kind)

    def sweep(par):
        loc[...] = fold(each_slot(q_s[...], pre, dot_nt))
        prev = loc[0:1]
        for j in range(1, CAP):
            parts = split3(prev)
            out = dot(parts, steps[j, 0]) + dot(parts, steps[j, 1])
            prev = loc[j : j + 1] + jnp.sum(out, axis=0, keepdims=True)
            loc[j : j + 1] = prev

        edge_loc = jnp.sum(dot(split3(loc[...]) * hot[0], low[0]), axis=0, keepdims=True)
        edge_buf[par] = edge_loc

    leave = jnp.where(first, other[...], ident)
    chip[...] = mm(
        mm(jnp.where(x < 1, xm[1], ident), jnp.where(x < 2, xm[2], ident)),
        jnp.where(x < 3, xm[3], ident),
    )
    tails[0] = ident
    tails[1] = leave
    own[...] = mm(leave, chip[...])
    tails[2] = own[...]
    tails[3] = own[...]
    hi, lo = split2(prefix[0])
    tails[4] = dot(hi, low[0]) + dot(lo, low[0])
    make_message(0)
    exchange_start(0)
    sweep(0)
    lax.fori_loop(12, CAP, join, 0)

    exchange_end(0)
    top = class_sums(0)[0][0]
    parts = split3(jnp.concatenate([top[0:1], top[1:2]], axis=1))
    hi, lo = split2(row[...])
    out = jnp.sum(dot(parts, hi) + dot(parts, lo), axis=0, keepdims=True)
    relay[...] = jnp.zeros_like(relay)
    relay[0:1] = out[:, :HALF]
    relay[1:2] = out[:, HALF:]
    relays = [
        remote(
            relay, relay_got, sl_sem.at[d - 1], rl_sem.at[0],
            lax.rem(t + d * 2 * NX, NT), s,
        )
        for d in (1, 2)
    ]

    @pl.when(y == 1)
    def _():
        for c in relays:
            c.start()

    swap = remote(ym.at[half], ym.at[half], sy_sem.at[1], ry_sem.at[1], mate, s)

    @pl.when(taker)
    def _():
        hop.wait_recv()
        swap.start()

    enter = jnp.where(first, ident, other[...])
    work[...] = mm(jnp.where(x > 1, xm[1], ident), jnp.where(x > 2, xm[2], ident))
    scans[2] = (enter * one(x > 0)).T
    behind = xm[lax.rem(x + 3, NX)]
    scans[3] = (mm(behind, enter) * one(x > 1)).T
    scans[4] = (mm(mm(xm[lax.rem(x + 2, NX)], behind), enter) * one(x > 2)).T
    scans[5] = ident * one(core > 0)
    work[...] = mm(mm(jnp.where(x > 0, xm[0], ident), work[...]), enter)
    scans[0] = (work[...] * one(y > 0)).T
    def flip_coup(j, _):
        coup_t[j] = flip(coup[j])
        return 0

    lax.fori_loop(0, CAP, flip_coup, 0, unroll=2)
    @pl.when(giver)
    def _():
        hop.wait_send()

    @pl.when(taker)
    def _():
        swap.wait()

    over = mm(jnp.where(y == 0, own[...], ym[...]), jnp.where(y == 0, ym[...], work[...]))
    scans[1] = (over * one(y == 3)).T
    tails[3] = jnp.where(y == 0, over, own[...])

    def iteration(k, _):
        par = lax.rem(k, 2)
        @pl.when(k > 0)
        def _():
            exchange_end(par)

        rows, cols, near = class_sums(par)
        sums = strips_start(par, rows, cols, near)
        rows[1] = jnp.where((k == 0) & (y == 2), relay_got[...], rows[1])
        rows[2] = jnp.where((k == 0) & (y == 3), relay_got[...], rows[2])
        heads = [rows[0] + rows[1] * one(y == 2), rows[1] + rows[2]] + cols + [near]
        to_column([(wide(h[0:1]), wide(h[1:2])) for h in heads], scans)
        for j in range(CAP):
            car[j : j + 1, :HALF], car[j : j + 1, HALF:] = to_row(prefix, j)
        step = (loc[...] + car[...]) * live
        up_buf[par] = step
        up = remote(
            up_buf.at[par], up_got.at[par], hs_sem.at[par, 0], hr_sem.at[par, 0],
            t, lax.rem(s + 1, NS),
        )
        up.start()
        left, right = to_row(tails, 4)
        edge_buf[par, :, :HALF] = edge_buf[par, :, :HALF] + left
        edge_buf[par, :, HALF:] = edge_buf[par, :, HALF:] + right
        edge = remote(
            edge_buf.at[par], edge_got.at[par], hs_sem.at[par, 1], hr_sem.at[par, 1],
            lax.rem(t + NT - 1, NT), s,
        )
        edge.start()
        down_buf[par] = fold(each_slot(step, coup))
        down = remote(
            down_buf.at[par], down_got.at[par], hs_sem.at[par, 2], hr_sem.at[par, 2],
            t, lax.rem(s + NS - 1, NS),
        )
        down.start()
        prevs[0:1, :HALF], prevs[0:1, HALF:] = to_row(tails, 0)
        shifts[0:CAP] = fold(each_slot(step, low))
        prevs[1 : CAP + 1] = step
        total = fold(each_slot(step, diag, dot_nt) + each_slot(prevs[0:CAP], low_t)) + shifts[1 : CAP + 1]
        alpha = strips_end(par, sums)
        alpha = jnp.broadcast_to(alpha, (CAP, W))
        start = k == 0
        r_s[...] = r_s[...] - jnp.where(start, 0.0, alpha * w_s[...])
        x_s[...] = x_s[...] + jnp.where(start, 0.0, alpha * z_s[...])
        z_s[...] = jnp.where(start, step, z_s[...] - alpha * step)
        up.wait_recv()
        zero = jnp.zeros((CAP, W), f32)
        below = jnp.where(s > 0, up_got[par], zero)
        total = total + fold(each_slot(below, coup_t))
        edge.wait_recv()
        down.wait_recv()
        total = total + jnp.where(s < NS - 1, down_got[par], zero)
        nxt = jnp.broadcast_to(edge_got[par], (CAP, W))
        total = (total + at_end * jnp.where(t < NT - 1, nxt, zero)) * live
        image = jnp.where(start, total, w_s[...] - alpha * total)
        w_s[...] = image
        q_s[...] = image
        for c in (up, edge, down):
            c.wait_send()
        send_end(par)
        put_sums(1 - par)

        @pl.when(k < ITERS - 1)
        def _():
            make_message(1 - par)
            exchange_start(1 - par)
            sweep(1 - par)

        @pl.when(k == ITERS - 1)
        def _():
            exchange_start(1 - par)

        return 0

    @pl.when(y == 1)
    def _():
        for c in relays:
            c.wait_send()

    @pl.when(y > 1)
    def _():
        relays[0].wait_recv()

    lax.fori_loop(0, ITERS, iteration, 0)
    par = ITERS % 2
    leaving = []
    for n, ref in enumerate((x_s, z_s, r_s, w_s)):
        c = pltpu.make_async_copy(ref, state_h.at[n], load_sem.at[n])
        c.start()
        leaving.append(c)
    exchange_end(par)
    alpha_out[...] = jnp.broadcast_to(strips_end(par, strips_start(par, *class_sums(par))), (CAP, W))
    send_end(par)
    for c in leaving:
        c.wait()


def body(rhs, diag, low, coup, pre, seg, links):
    vmem = pl.BlockSpec(memory_space=pltpu.VMEM)
    smem = pl.BlockSpec(memory_space=pltpu.SMEM)
    anyw = pl.BlockSpec(memory_space=pl.ANY)
    mats = pltpu.VMEM((CAP, W, W), bf16)
    mats2 = pltpu.VMEM((CAP, 2, W, W), bf16)
    big = pltpu.VMEM((W, W), f32)
    big4 = pltpu.VMEM((4, W, W), f32)
    vec = pltpu.VMEM((CAP, W), f32)
    dma = pltpu.SemaphoreType.DMA
    out = jax.ShapeDtypeStruct((CAP, W), f32)
    state, alpha = pl.pallas_call(
        kernel,
        out_shape=(jax.ShapeDtypeStruct((4, CAP, W), f32), out),
        in_specs=[smem, smem, vmem, anyw, anyw, anyw, anyw],
        out_specs=(anyw, vmem),
        scratch_shapes=[mats] * 6
        + [
            mats2, pltpu.VMEM((CAP, W, W), f32), pltpu.VMEM((CAP, W, W), f32),
            pltpu.VMEM((6, W, W), f32), pltpu.VMEM((5, W, W), f32),
            big, big, big, big4, big, big, big, big,
            pltpu.VMEM((CAP, 48, W), bf16),
            pltpu.VMEM((2, 4, 4, HALF), f32), pltpu.VMEM((2, NT - 1, 4, HALF), f32),
            pltpu.VMEM((2, 4, HALF), f32), pltpu.VMEM((2, NS - 1, 4, HALF), f32),
            pltpu.VMEM((2, CAP, W), f32), pltpu.VMEM((2, CAP, W), f32),
            pltpu.VMEM((2, CAP, W), f32), pltpu.VMEM((2, CAP, W), f32),
            pltpu.VMEM((2, 1, W), f32), pltpu.VMEM((2, 1, W), f32),
            pltpu.VMEM((3, W, W), f32), pltpu.VMEM((W, HALF), f32), vec,
            vec, pltpu.VMEM((CAP + 8, W), f32), pltpu.VMEM((CAP + 8, W), f32),
            vec, vec, vec, vec, vec,
            dma((10,)), dma((2,)), dma((3,)), dma((3,)), dma((3,)), dma((3,)), dma((2,)), dma((2,)),
            dma((2,)), dma((2,)), dma((2, 3)), dma((2, 3)), dma((2, 3)), dma((2, 3)),
            pltpu.VMEM((4, HALF), f32), pltpu.VMEM((4, HALF), f32), dma((2,)), dma((1,)),
        ],
        compiler_params=pltpu.CompilerParams(
            collective_id=0, has_side_effects=True, vmem_limit_bytes=58 * 1024 * 1024
        ),
        name="solve",
    )(seg, links, rhs[0], diag[0], low[0], coup[0], pre[0])
    sol = state[0] + alpha * state[1]
    res = state[2] - alpha * state[3]
    return sol[None], res[None]


def solution(mesh):
    in_specs = (
        P("strip", "track", None),
        P("strip", "track", None, None),
        P("strip", "track", None, None),
        P("strip", "track", None, None),
        P("strip", "track", None, None),
        P("track"),
        P("strip", "track"),
    )
    out_specs = (P("strip", "track", None), P("strip", "track", None))
    return jax.shard_map(body, mesh=mesh, in_specs=in_specs, out_specs=out_specs, check_vma=False)
```
